128 devices in a mesh: inb: 16 (over x, y), outb: 8 (over z, core).
Axes of the slice: x: 4, y: 4, z: 4, core: 2. Of those that a mesh axis runs over, the one named last changes fastest.
Arguments:
- tokens: bfloat16 [1024, 12288], P('outb', 'inb'), may hold values from -6 to 6
- weight_blocks: bfloat16 [16, 8, 72, 128, 128], P('inb', 'outb'), may hold values from -0.15625 to 0.15625
- block_rows: int32 [16, 8, 72], P('inb', 'outb'), may hold values from 0 to 95, as said below
- block_cols: int32 [16, 8, 72], P('inb', 'outb'), may hold values from 0 to 383, as said below
- block_count: int32 [16, 8], P('inb', 'outb'), may hold values from 9 to 72, as said below
- grad_act: bfloat16 [1024, 49152], P('inb', 'outb'), may hold values from -6 to 6
Outputs:
- activation: bfloat16 [1024, 49152], P('inb', 'outb')
- grad_tokens: float32 [1024, 12288], P('outb', 'inb')
- grad_weights: float32 [16, 8, 72, 128, 128], P('inb', 'outb')
The draws below stay inside these ranges and needn't reach their ends.
Inputs may be any that keep to these rules, and one draw needn't show every extreme that they name: block_rows[a, b, s] lies in owner a's input blocks and block_cols[a, b, s] in owner b's hidden blocks; the slots of one owner name distinct blocks, dead slots included. `block_cols`: see block_rows. `block_count`: at least one owner has all 72 slots live.
All inputs are finite; a program needn't handle non-finite values.
Results may differ from the reference program's by a relative error of at most 0.02.
Values may be sent and summed in bfloat16 or wider, within the bound.
A program may use at most 192 MiB of HBM per device.

```python
import jax
import jax.numpy as jnp
from jax import lax

D = 12288
H = 49152
BLK = 128
TOKENS = 1024
ROWS_DEV = 6
COLS_DEV = 48
CAP = 72
N_INB = 16
N_OUTB = 8


def pattern(key):
    owner_total = N_INB * N_OUTB
    cell_total = ROWS_DEV * COLS_DEV
    base = jax.random.fold_in(key, 11)
    owner_keys = jax.random.split(base, owner_total)
    chosen = jax.vmap(lambda owner_key: jax.random.permutation(owner_key, cell_total)[:CAP])(owner_keys)
    chosen = chosen.astype(jnp.int32).reshape(N_INB, N_OUTB, CAP)
    counts = jax.random.randint(jax.random.fold_in(key, 12), (owner_total,), CAP // 8, CAP * 7 // 8 + 1, dtype=jnp.int32)
    fullest = jax.random.randint(jax.random.fold_in(key, 13), (), 0, owner_total, dtype=jnp.int32)
    counts = jnp.where(jnp.arange(owner_total, dtype=jnp.int32) == fullest, CAP, counts).reshape(N_INB, N_OUTB)
    row_position_index = chosen // COLS_DEV + jnp.arange(N_INB, dtype=jnp.int32)[:, None, None] * ROWS_DEV
    col_index = chosen % COLS_DEV + jnp.arange(N_OUTB, dtype=jnp.int32)[None, :, None] * COLS_DEV
    return (row_position_index.astype(jnp.int32), col_index.astype(jnp.int32), counts.astype(jnp.int32))


def draw_block_rows(key, part):
    return pattern(key)[0]


def draw_block_cols(key, part):
    return pattern(key)[1]


def draw_block_count(key, part):
    return pattern(key)[2]


def block_levels(own_key, shape, cuts, least, largest):
    gain = 1.0
    for axis_at, blocks in cuts:
        steps = jax.random.uniform(jax.random.fold_in(jax.random.fold_in(own_key, 6), axis_at), (blocks,), jnp.float32, least / len(cuts), largest / len(cuts))
        gain = gain * jnp.repeat(jnp.exp(steps), shape[axis_at] // blocks).reshape((-1,) + (1,) * (len(shape) - 1 - axis_at))
    return gain


def bell_draw(key, extent, width, limit, shards=(), held_as=jnp.bfloat16):
    entries = width * jax.random.normal(key, extent, jnp.float32)
    if shards:
        entries = entries * block_levels(key, extent, shards, -0.22, 0.18)
    return jnp.clip(entries, -limit, limit).astype(held_as)


def setup_inputs(seed: int = 0) -> dict:
    key_list = jax.random.split(jax.random.key(seed), 7)
    tokens = bell_draw(key_list[0], (TOKENS, D), 1.0, 6.0, ((0, 8), (1, 16)))
    weight_blocks = bell_draw(key_list[1], (N_INB, N_OUTB, CAP, BLK, BLK), (D // 8) ** -0.5, 0.15625, ((0, 16), (1, 8)))
    block_rows = draw_block_rows(jax.random.fold_in(key_list[6], 71), 0)
    block_cols = draw_block_cols(jax.random.fold_in(key_list[6], 71), 0)
    block_count = draw_block_count(jax.random.fold_in(key_list[6], 71), 0)
    grad_act = bell_draw(key_list[5], (TOKENS, H), 1.0, 6.0, ((0, 16), (1, 8)))
    return dict(tokens=tokens, weight_blocks=weight_blocks, block_rows=block_rows, block_cols=block_cols, block_count=block_count, grad_act=grad_act)


inv_root_two = 0.7071067811865476
inv_root_tau = 0.3989422804014327


def gelu_slope(values):
    normal_cdf = 0.5 * (1.0 + jax.scipy.special.erf(values * inv_root_two))
    return normal_cdf + values * jnp.exp(-0.5 * values * values) * inv_root_tau


def owner_forward(x_cols, weights, row_local, col_local, is_live, column_block_list):
    token_count = x_cols.shape[0]
    block_size = weights.shape[-1]
    input_blocks = jnp.take(x_cols.reshape(token_count, -1, block_size), row_local, axis=1).astype(jnp.float32)
    products = jnp.einsum("tcf,cfh->tch", input_blocks, weights.astype(jnp.float32), precision=lax.Precision.HIGHEST)
    placing = ((col_local[:, None] == jnp.arange(column_block_list, dtype=jnp.int32)[None, :]) & is_live[:, None]).astype(jnp.float32)
    summed = jnp.einsum("tch,cj->tjh", products, placing, precision=lax.Precision.HIGHEST)
    return summed.reshape(token_count, column_block_list * block_size)


def reference(tokens, weight_blocks, block_rows, block_cols, block_count, grad_act):
    slot_ids = jnp.arange(CAP, dtype=jnp.int32)

    def forward_step(running, row_owner):
        x_cols = lax.dynamic_slice_in_dim(tokens, row_owner * (ROWS_DEV * BLK), ROWS_DEV * BLK, 1)
        pieces = []
        for column_owner in range(N_OUTB):
            row_local = block_rows[row_owner, column_owner] - row_owner * ROWS_DEV
            col_local = block_cols[row_owner, column_owner] - column_owner * COLS_DEV
            is_live = slot_ids < block_count[row_owner, column_owner]
            pieces.append(owner_forward(x_cols, weight_blocks[row_owner, column_owner], row_local, col_local, is_live, COLS_DEV).astype(jnp.bfloat16))
        rounded = lax.optimization_barrier(jnp.concatenate(pieces, axis=1))
        return running + rounded.astype(jnp.float32), None

    preact, _ = lax.scan(forward_step, jnp.zeros((TOKENS, H), jnp.float32), jnp.arange(N_INB, dtype=jnp.int32))
    activation = jax.nn.gelu(preact, approximate=False).astype(jnp.bfloat16)
    grad_pre = (grad_act.astype(jnp.float32) * gelu_slope(preact)).astype(jnp.bfloat16)

    def backward_step(carry, row_owner):
        x_cols = lax.dynamic_slice_in_dim(tokens, row_owner * (ROWS_DEV * BLK), ROWS_DEV * BLK, 1)
        input_segments = x_cols.reshape(TOKENS, ROWS_DEV, BLK)
        input_gradient = jnp.zeros((TOKENS, ROWS_DEV, BLK), jnp.float32)
        weight_list = []
        for column_owner in range(N_OUTB):
            row_local = block_rows[row_owner, column_owner] - row_owner * ROWS_DEV
            col_local = block_cols[row_owner, column_owner] - column_owner * COLS_DEV
            is_live = slot_ids < block_count[row_owner, column_owner]
            weights = weight_blocks[row_owner, column_owner].astype(jnp.float32)
            grad_cols = grad_pre[:, column_owner * COLS_DEV * BLK:(column_owner + 1) * COLS_DEV * BLK]
            grad_blocks = jnp.take(grad_cols.reshape(TOKENS, COLS_DEV, BLK), col_local, axis=1).astype(jnp.float32)
            input_blocks = jnp.take(input_segments, row_local, axis=1).astype(jnp.float32)
            final_output = jnp.einsum("tch,cfh->tcf", grad_blocks, weights, precision=lax.Precision.HIGHEST)
            row_assignment = ((row_local[:, None] == jnp.arange(ROWS_DEV, dtype=jnp.int32)[None, :]) & is_live[:, None]).astype(jnp.float32)
            input_gradient = input_gradient + jnp.einsum("hgk,gw->hwk", final_output, row_assignment, precision=lax.Precision.HIGHEST)
            slot_grad = jnp.einsum("tcf,tch->cfh", input_blocks, grad_blocks, precision=lax.Precision.HIGHEST)
            weight_list.append(slot_grad * is_live[:, None, None].astype(jnp.float32))
        return carry, (input_gradient.reshape(TOKENS, ROWS_DEV * BLK), jnp.stack(weight_list))

    _, (gradient_groups, grad_weights) = lax.scan(backward_step, jnp.zeros((), jnp.float32), jnp.arange(N_INB, dtype=jnp.int32))
    grad_tokens = jnp.transpose(gradient_groups, (1, 0, 2)).reshape(TOKENS, D)
    return activation, grad_tokens, grad_weights
```

```python
import functools

import jax
import jax.numpy as jnp
from jax import lax
from jax.experimental import pallas as pl
from jax.experimental.pallas import tpu as pltpu
from jax.sharding import PartitionSpec as P

MESH = pl.DeviceIdType.MESH
F32 = jnp.float32
BF16 = jnp.bfloat16
INV_ROOT_TWO = 0.7071067811865476
INV_ROOT_TAU = 0.3989422804014327
BLK = 128
RB = 6
CBK = 48
CAP = 72
WB = 2
W = WB * BLK
NCH = CBK // (2 * WB)
SL = 4


def add2(a, b):
    return (a.astype(F32) + b.astype(F32)).astype(BF16)


def kernel(
    idx, cell, live, tok, wblk, gact,
    act, dx_out, gw_out,
    wp, xs, xt, ps, r1, r2, qs, t1, t2, gs, dxa, gw, sb, sr, eb, u1, u2,
    ssem, rsem, asem, arsem, lsem,
):
    a = lax.axis_index("inb")
    b = lax.axis_index("outb")
    x, y = a // 4, a % 4
    z, c = b // 2, b % 2

    def up(v):
        return lax.rem(v + 1, 4)

    def down(v):
        return lax.rem(v + 3, 4)

    def opp(v):
        return lax.rem(v + 2, 4)

    zr, zl, zo = up(z), down(z), opp(z)
    sib = (a, 2 * z + (1 - c))
    zr_dev, zl_dev = (a, 2 * zr + c), (a, 2 * zl + c)

    first = (x, y)
    second = (y, x)

    def dev_first(t, v):
        return (4 * v + y, b) if t == 0 else (4 * x + v, b)

    def dev_second(t, v):
        return (4 * x + v, b) if t == 0 else (4 * v + y, b)

    wcopy = pltpu.make_async_copy(wblk, wp.at[pl.ds(0, CAP)], lsem.at[0])
    wcopy.start()
    xcopy = pltpu.make_async_copy(tok, xs.at[b], lsem.at[1])
    xcopy.start()

    barrier = pltpu.get_barrier_semaphore()
    for dev in (
        dev_first(0, up(x)), dev_first(0, down(x)),
        dev_first(1, up(y)), dev_first(1, down(y)),
        zr_dev, zl_dev, sib,
    ):
        pl.semaphore_signal(barrier, inc=1, device_id=dev, device_id_type=MESH)
    wp[CAP] = jnp.zeros((BLK, BLK), BF16)
    pl.semaphore_wait(barrier, 7)

    def ac(n, src, dst, dev):
        return pltpu.make_async_remote_copy(
            src_ref=src, dst_ref=dst, send_sem=asem.at[n], recv_sem=arsem.at[n],
            device_id=dev, device_id_type=MESH,
        )

    def xb(zz, cc):
        return xs.at[2 * zz + cc]

    def xh(zz, cc, h):
        return xs.at[2 * zz + cc, pl.ds(64 * h, 64)]

    sends = []

    def go(n, src, dst, dev):
        d = ac(n, src, dst, dev)
        d.start()
        sends.append(d)

    def got(n, dst):
        ac(n, dst, dst, sib).wait_recv()

    go(0, tok, xb(z, c), zr_dev)
    go(1, tok, xb(z, c), zl_dev)
    go(2, tok, xb(z, c), sib)
    got(0, xb(zl, c))
    go(3, xh(zl, c, 0), xh(zl, c, 0), zr_dev)
    got(1, xb(zr, c))
    go(4, xh(zr, c, 1), xh(zr, c, 1), zl_dev)
    go(5, xb(zl, c), xb(zl, c), sib)
    go(6, xb(zr, c), xb(zr, c), sib)
    got(3, xh(zo, c, 0))
    go(7, xh(zo, c, 0), xh(zo, c, 0), sib)
    got(4, xh(zo, c, 1))
    go(8, xh(zo, c, 1), xh(zo, c, 1), sib)
    xcopy.wait()
    wcopy.wait()
    got(2, xb(z, 1 - c))
    got(5, xb(zl, 1 - c))
    got(6, xb(zr, 1 - c))
    got(7, xh(zo, 1 - c, 0))
    got(8, xh(zo, 1 - c, 1))
    for d in sends:
        d.wait_send()

    dxa[...] = jnp.zeros_like(dxa)
    for r in range(RB):
        for q in range(8):
            xt[r * BLK:(r + 1) * BLK, q * BLK:(q + 1) * BLK] = xs[q, :, r * BLK:(r + 1) * BLK].T

    def weights(k):
        cols = []
        for j in range(2 * WB):
            col = 2 * WB * k + j
            cols.append(jnp.concatenate([wp[idx[r * CBK + col]] for r in range(RB)], axis=0))
        return jnp.concatenate(cols, axis=1)

    def copy(k, t, n, src, dst, dev):
        slot = lax.rem(k, SL)
        return pltpu.make_async_remote_copy(
            src_ref=src, dst_ref=dst,
            send_sem=ssem.at[slot, t, n], recv_sem=rsem.at[slot, t, n],
            device_id=dev, device_id_type=MESH,
        )

    def start(k, t, n, src, dst, dev):
        copy(k, t, n, src, dst, dev).start()

    def arrived(k, t, n, dst):
        copy(k, t, n, dst, dst, sib).wait_recv()

    def sent(k, t, n, src):
        copy(k, t, n, src, src, sib).wait_send()

    def stage0(k):
        slot = lax.rem(k, SL)
        rhs = weights(k)
        for m in range(4):
            lhs = jnp.concatenate([xs[2 * m], xs[2 * m + 1]], axis=0)
            out = jnp.dot(lhs, rhs, preferred_element_type=F32).astype(BF16)
            for n in range(4):
                ps[slot, 0, m, n] = out[64 * n:64 * n + 64, :W]
                ps[slot, 1, n, m] = out[64 * n:64 * n + 64, W:]
        for t in range(2):
            f = first[t]
            r, l, o = up(f), down(f), opp(f)
            lo, hi = pl.ds(0, 2), pl.ds(2, 2)
            start(k, t, 0, ps.at[slot, t, o, lo], r1.at[slot, t, 0], dev_first(t, r))
            start(k, t, 1, ps.at[slot, t, o, hi], r1.at[slot, t, 1], dev_first(t, l))
            start(k, t, 2, ps.at[slot, t, r, hi], r2.at[slot, t, 0, hi], dev_first(t, r))
            start(k, t, 3, ps.at[slot, t, l, lo], r2.at[slot, t, 1, lo], dev_first(t, l))

    def stage1(k):
        slot = lax.rem(k, SL)
        for t in range(2):
            f = first[t]
            r, l = up(f), down(f)
            lo, hi = pl.ds(0, 2), pl.ds(2, 2)
            arrived(k, t, 0, r1.at[slot, t, 0])
            ps[slot, t, r, lo] = add2(ps[slot, t, r, lo], r1[slot, t, 0])
            start(k, t, 4, ps.at[slot, t, r, lo], r2.at[slot, t, 0, lo], dev_first(t, r))
            arrived(k, t, 1, r1.at[slot, t, 1])
            ps[slot, t, l, hi] = add2(ps[slot, t, l, hi], r1[slot, t, 1])
            start(k, t, 5, ps.at[slot, t, l, hi], r2.at[slot, t, 1, hi], dev_first(t, l))

    def stage2(k):
        slot = lax.rem(k, SL)
        for t in range(2):
            f, s = first[t], second[t]
            lo, hi = pl.ds(0, 2), pl.ds(2, 2)
            arrived(k, t, 2, r2.at[slot, t, 0, hi])
            arrived(k, t, 3, r2.at[slot, t, 1, lo])
            arrived(k, t, 4, r2.at[slot, t, 0, lo])
            arrived(k, t, 5, r2.at[slot, t, 1, hi])
            qs[slot, t] = (
                ps[slot, t, f].astype(F32) + r2[slot, t, 0].astype(F32) + r2[slot, t, 1].astype(F32)
            ).astype(BF16)
            for n in range(6):
                sent(k, t, n, r1.at[slot, t, 0])
            r, l, o = up(s), down(s), opp(s)
            lo, hi = pl.ds(0, 32), pl.ds(32, 32)
            start(k, t, 6, qs.at[slot, t, o, lo], t1.at[slot, t, 0], dev_second(t, r))
            start(k, t, 7, qs.at[slot, t, o, hi], t1.at[slot, t, 1], dev_second(t, l))
            start(k, t, 8, qs.at[slot, t, r, hi], t2.at[slot, t, 0, hi], dev_second(t, r))
            start(k, t, 9, qs.at[slot, t, l, lo], t2.at[slot, t, 1, lo], dev_second(t, l))

    def stage3(k):
        slot = lax.rem(k, SL)
        for t in range(2):
            s = second[t]
            r, l = up(s), down(s)
            lo, hi = pl.ds(0, 32), pl.ds(32, 32)
            arrived(k, t, 6, t1.at[slot, t, 0])
            qs[slot, t, r, lo] = add2(qs[slot, t, r, lo], t1[slot, t, 0])
            start(k, t, 10, qs.at[slot, t, r, lo], t2.at[slot, t, 0, lo], dev_second(t, r))
            arrived(k, t, 7, t1.at[slot, t, 1])
            qs[slot, t, l, hi] = add2(qs[slot, t, l, hi], t1[slot, t, 1])
            start(k, t, 11, qs.at[slot, t, l, hi], t2.at[slot, t, 1, hi], dev_second(t, l))

    def stage4(k):
        slot = lax.rem(k, SL)
        for t in range(2):
            f, s = first[t], second[t]
            lo, hi = pl.ds(0, 32), pl.ds(32, 32)
            arrived(k, t, 8, t2.at[slot, t, 0, hi])
            arrived(k, t, 9, t2.at[slot, t, 1, lo])
            arrived(k, t, 10, t2.at[slot, t, 0, lo])
            arrived(k, t, 11, t2.at[slot, t, 1, hi])
            pre = qs[slot, t, s].astype(F32) + t2[slot, t, 0].astype(F32) + t2[slot, t, 1].astype(F32)
            cdf = 0.5 * (1.0 + lax.erf(pre * INV_ROOT_TWO))
            cols = pl.ds(pl.multiple_of((2 * k + t) * W, W), W)
            act[:, cols] = (pre * cdf).astype(BF16)
            slope = cdf + pre * jnp.exp(-0.5 * pre * pre) * INV_ROOT_TAU
            gs[k, t, f, s] = (gact[:, cols].astype(F32) * slope).astype(BF16)
            for n in range(6, 12):
                sent(k, t, n, t1.at[slot, t, 0])
            start(k, t, 12, gs.at[k, t, f, s], gs.at[k, t, f, s], dev_second(t, up(s)))
            start(k, t, 13, gs.at[k, t, f, s], gs.at[k, t, f, s], dev_second(t, down(s)))

    def stage5(k):
        for t in range(2):
            f, s = first[t], second[t]
            r, l = up(s), down(s)
            lo, hi = pl.ds(0, 32), pl.ds(32, 32)
            arrived(k, t, 12, gs.at[k, t, f, l])
            start(k, t, 14, gs.at[k, t, f, l, lo], gs.at[k, t, f, l, lo], dev_second(t, r))
            arrived(k, t, 13, gs.at[k, t, f, r])
            start(k, t, 15, gs.at[k, t, f, r, hi], gs.at[k, t, f, r, hi], dev_second(t, l))

    def stage6(k):
        for t in range(2):
            f, s = first[t], second[t]
            o = opp(s)
            lo, hi = pl.ds(0, 32), pl.ds(32, 32)
            arrived(k, t, 14, gs.at[k, t, f, o, lo])
            arrived(k, t, 15, gs.at[k, t, f, o, hi])
            start(k, t, 16, gs.at[k, t, f], gs.at[k, t, f], dev_first(t, up(f)))
            start(k, t, 17, gs.at[k, t, f], gs.at[k, t, f], dev_first(t, down(f)))

    def stage7(k):
        for t in range(2):
            f = first[t]
            r, l = up(f), down(f)
            lo, hi = pl.ds(0, 2), pl.ds(2, 2)
            arrived(k, t, 16, gs.at[k, t, l])
            start(k, t, 18, gs.at[k, t, l, lo], gs.at[k, t, l, lo], dev_first(t, r))
            arrived(k, t, 17, gs.at[k, t, r])
            start(k, t, 19, gs.at[k, t, r, hi], gs.at[k, t, r, hi], dev_first(t, l))

    def stage8(k):
        for t in range(2):
            f, s = first[t], second[t]
            o = opp(f)
            lo, hi = pl.ds(0, 2), pl.ds(2, 2)
            arrived(k, t, 18, gs.at[k, t, o, lo])
            arrived(k, t, 19, gs.at[k, t, o, hi])
            sent(k, t, 12, gs.at[k, t, f, s])
            sent(k, t, 13, gs.at[k, t, f, s])
            sent(k, t, 14, gs.at[k, t, f, s, pl.ds(0, 32)])
            sent(k, t, 15, gs.at[k, t, f, s, pl.ds(0, 32)])
            sent(k, t, 16, gs.at[k, t, f])
            sent(k, t, 17, gs.at[k, t, f])
            sent(k, t, 18, gs.at[k, t, o, lo])
            sent(k, t, 19, gs.at[k, t, o, hi])
        rhs = weights(k)
        g0 = jnp.concatenate([gs[k, 0, n // 4, n % 4] for n in range(16)], axis=0)
        g1 = jnp.concatenate([gs[k, 1, n % 4, n // 4] for n in range(16)], axis=0)
        g = jnp.concatenate([g0, g1], axis=1)
        term = lax.dot_general(g, rhs, (((1,), (1,)), ((), ())), preferred_element_type=F32)
        dxa[...] += term.reshape(8, BLK, RB * BLK)
        wg = jnp.dot(xt[...], g, preferred_element_type=F32)
        for r in range(RB):
            for j in range(2 * WB):
                gw[r * CBK + 2 * WB * k + j] = wg[r * BLK:(r + 1) * BLK, j * BLK:(j + 1) * BLK]

    stages = (stage0, stage1, stage2, stage3, stage4, stage5, stage6, stage7, stage8)

    def body(i, carry):
        for n in range(len(stages) - 1, -1, -1):
            k = i - n

            @pl.when((k >= 0) & (k < NCH))
            def _():
                stages[n](k)

        return carry

    lax.fori_loop(0, NCH + len(stages) - 1, body, 0)

    sends.clear()
    for q in range(4):
        sb[q] = dxa[2 * q + (1 - c)].astype(BF16)
    go(9, sb, sr, sib)

    def extract(s, carry):
        gw_out[s] = gw[cell[s]] * live[s]
        return carry

    got(9, sr)
    for q in range(4):
        eb[q] = (dxa[2 * q + c] + sr[q].astype(F32)).astype(BF16)
    lo, hi = pl.ds(0, 64), pl.ds(64, 64)
    go(10, eb.at[zo, lo], u1.at[0], zr_dev)
    go(11, eb.at[zo, hi], u1.at[1], zl_dev)
    go(12, eb.at[zr, hi], u2.at[0, hi], zr_dev)
    go(13, eb.at[zl, lo], u2.at[1, lo], zl_dev)
    lax.fori_loop(0, CAP // 2, extract, 0)
    got(10, u1.at[0])
    eb[zr, lo] = add2(eb[zr, lo], u1[0])
    go(14, eb.at[zr, lo], u2.at[0, lo], zr_dev)
    got(11, u1.at[1])
    eb[zl, hi] = add2(eb[zl, hi], u1[1])
    go(15, eb.at[zl, hi], u2.at[1, hi], zl_dev)
    lax.fori_loop(CAP // 2, CAP, extract, 0)
    got(12, u2.at[0, hi])
    got(13, u2.at[1, lo])
    got(14, u2.at[0, lo])
    got(15, u2.at[1, hi])
    dx_out[...] = eb[z].astype(F32) + u2[0].astype(F32) + u2[1].astype(F32)
    for d in sends:
        d.wait_send()


def per_device(tokens, weight_blocks, block_rows, block_cols, block_count, grad_act):
    slot_ids = jnp.arange(CAP, dtype=jnp.int32)
    row_local = block_rows[0, 0] - lax.axis_index("inb") * RB
    col_local = block_cols[0, 0] - lax.axis_index("outb") * CBK
    is_live = slot_ids < block_count[0, 0]
    cell = row_local * CBK + col_local
    hit = (jnp.arange(RB * CBK, dtype=jnp.int32)[:, None] == cell[None, :]) & is_live[None, :]
    idx = CAP - jnp.sum(jnp.where(hit, CAP - slot_ids[None, :], 0), axis=1)
    vmem = pl.BlockSpec(memory_space=pltpu.VMEM)
    smem = pl.BlockSpec(memory_space=pltpu.SMEM)
    out = pl.pallas_call(
        kernel,
        out_shape=(
            jax.ShapeDtypeStruct((64, CBK * BLK), BF16),
            jax.ShapeDtypeStruct((BLK, RB * BLK), F32),
            jax.ShapeDtypeStruct((CAP, BLK, BLK), F32),
        ),
        in_specs=[smem, smem, smem, vmem, pl.BlockSpec(memory_space=pl.ANY), vmem],
        out_specs=(vmem, vmem, vmem),
        scratch_shapes=[
            pltpu.VMEM((CAP + 1, BLK, BLK), BF16),
            pltpu.VMEM((8, BLK, RB * BLK), BF16),
            pltpu.VMEM((RB * BLK, 1024), BF16),
            pltpu.VMEM((SL, 2, 4, 4, 64, W), BF16),
            pltpu.VMEM((SL, 2, 2, 2, 64, W), BF16),
            pltpu.VMEM((SL, 2, 2, 4, 64, W), BF16),
            pltpu.VMEM((SL, 2, 4, 64, W), BF16),
            pltpu.VMEM((SL, 2, 2, 32, W), BF16),
            pltpu.VMEM((SL, 2, 2, 64, W), BF16),
            pltpu.VMEM((NCH, 2, 4, 4, 64, W), BF16),
            pltpu.VMEM((8, BLK, RB * BLK), F32),
            pltpu.VMEM((RB * CBK, BLK, BLK), F32),
            pltpu.VMEM((4, BLK, RB * BLK), BF16),
            pltpu.VMEM((4, BLK, RB * BLK), BF16),
            pltpu.VMEM((4, BLK, RB * BLK), BF16),
            pltpu.VMEM((2, 64, RB * BLK), BF16),
            pltpu.VMEM((2, BLK, RB * BLK), BF16),
            pltpu.SemaphoreType.DMA((SL, 2, 20)),
            pltpu.SemaphoreType.DMA((SL, 2, 20)),
            pltpu.SemaphoreType.DMA((16,)),
            pltpu.SemaphoreType.DMA((16,)),
            pltpu.SemaphoreType.DMA((2,)),
        ],
        compiler_params=pltpu.CompilerParams(
            collective_id=0, has_side_effects=True, vmem_limit_bytes=67043328
        ),
        name="ffn",
    )(idx, cell, is_live.astype(F32), tokens, weight_blocks[0, 0], grad_act)
    activation, grad_tokens, grad_weights = out
    return (activation, grad_tokens, grad_weights[None, None])


def solution(mesh):
    in_specs = (
        P("outb", "inb"),
        P("inb", "outb", None, None, None),
        P("inb", "outb", None),
        P("inb", "outb", None),
        P("inb", "outb"),
        P("inb", "outb"),
    )
    out_specs = (P("inb", "outb"), P("outb", "inb"), P("inb", "outb", None, None, None))
    return jax.shard_map(
        per_device, mesh=mesh, in_specs=in_specs, out_specs=out_specs, check_vma=False
    )
```

```python
import functools

import jax
import jax.numpy as jnp
from jax import lax
from jax.experimental import pallas as pl
from jax.experimental.pallas import tpu as pltpu
from jax.sharding import PartitionSpec as P

MESH = pl.DeviceIdType.MESH
F32 = jnp.float32
BF16 = jnp.bfloat16
INV_ROOT_TWO = 0.7071067811865476
INV_ROOT_TAU = 0.3989422804014327
BLK = 128
RB = 6
CBK = 48
CAP = 72
WB = 2
W = WB * BLK
NCH = CBK // (2 * WB)
SL = 4


def add2(a, b):
    return (a.astype(F32) + b.astype(F32)).astype(BF16)


def kernel(
    idx, tok, wblk, gact_hbm,
    act_hbm, dx_out, gw_hbm,
    wp, xs, xt, ps, r1, r2, qs, t1, t2, gs, dxa, gact, act, gwst, sb, sr, eb, u1, u2,
    ssem, rsem, asem, arsem, lsem, osem, gsem,
):
    a = lax.axis_index("inb")
    b = lax.axis_index("outb")
    x, y = a // 4, a % 4
    z, c = b // 2, b % 2

    def up(v):
        return lax.rem(v + 1, 4)

    def down(v):
        return lax.rem(v + 3, 4)

    def opp(v):
        return lax.rem(v + 2, 4)

    zr, zl, zo = up(z), down(z), opp(z)
    sib = (a, 2 * z + (1 - c))
    zr_dev, zl_dev = (a, 2 * zr + c), (a, 2 * zl + c)

    first = (x, y)
    second = (y, x)

    def dev_first(t, v):
        return (4 * v + y, b) if t == 0 else (4 * x + v, b)

    def dev_second(t, v):
        return (4 * x + v, b) if t == 0 else (4 * v + y, b)

    wcopy = pltpu.make_async_copy(wblk, wp.at[pl.ds(0, CAP)], lsem.at[0])
    wcopy.start()
    xcopy = pltpu.make_async_copy(tok, xs.at[b], lsem.at[1])
    xcopy.start()
    gcopy = pltpu.make_async_copy(gact_hbm, gact, lsem.at[2])
    gcopy.start()

    barrier = pltpu.get_barrier_semaphore()
    for dev in (
        dev_first(0, up(x)), dev_first(0, down(x)),
        dev_first(1, up(y)), dev_first(1, down(y)),
        zr_dev, zl_dev, sib,
    ):
        pl.semaphore_signal(barrier, inc=1, device_id=dev, device_id_type=MESH)
    wp[CAP] = jnp.zeros((BLK, BLK), BF16)
    pl.semaphore_wait(barrier, 7)

    def ac(n, src, dst, dev):
        return pltpu.make_async_remote_copy(
            src_ref=src, dst_ref=dst, send_sem=asem.at[n], recv_sem=arsem.at[n],
            device_id=dev, device_id_type=MESH,
        )

    def xb(zz, cc):
        return xs.at[2 * zz + cc]

    def xh(zz, cc, h):
        return xs.at[2 * zz + cc, pl.ds(64 * h, 64)]

    sends = []

    def go(n, src, dst, dev):
        d = ac(n, src, dst, dev)
        d.start()
        sends.append(d)

    def got(n, dst):
        ac(n, dst, dst, sib).wait_recv()

    th = [tok.at[pl.ds(0, 64)], tok.at[pl.ds(64, 64)]]
    go(0, th[0], xh(z, c, 0), zr_dev)
    go(1, th[1], xh(z, c, 1), zl_dev)
    go(2, th[1], xh(z, c, 1), zr_dev)
    go(3, th[0], xh(z, c, 0), zl_dev)
    go(4, tok, xb(z, c), sib)
    dxa[...] = jnp.zeros_like(dxa)
    got(0, xh(zl, c, 0))
    go(5, xh(zl, c, 0), xh(zl, c, 0), zr_dev)
    got(1, xh(zr, c, 1))
    go(6, xh(zr, c, 1), xh(zr, c, 1), zl_dev)
    go(7, xh(zl, c, 0), xh(zl, c, 0), sib)
    go(8, xh(zr, c, 1), xh(zr, c, 1), sib)
    xcopy.wait()
    wcopy.wait()
    got(4, xb(z, 1 - c))

    def weights(k):
        cols = []
        for j in range(2 * WB):
            col = 2 * WB * k + j
            cols.append(jnp.concatenate([wp[idx[r * CBK + col]] for r in range(RB)], axis=0))
        return jnp.concatenate(cols, axis=1)

    def copy(k, t, n, src, dst, dev):
        slot = lax.rem(k, SL)
        return pltpu.make_async_remote_copy(
            src_ref=src, dst_ref=dst,
            send_sem=ssem.at[slot, t, n], recv_sem=rsem.at[slot, t, n],
            device_id=dev, device_id_type=MESH,
        )

    def start(k, t, n, src, dst, dev):
        copy(k, t, n, src, dst, dev).start()

    def arrived(k, t, n, dst):
        copy(k, t, n, dst, dst, sib).wait_recv()

    def sent(k, t, n, src):
        copy(k, t, n, src, src, sib).wait_send()

    def rows(slot, m, rhs):
        lhs = jnp.concatenate([xs[2 * m], xs[2 * m + 1]], axis=0)
        out = jnp.dot(lhs, rhs, preferred_element_type=F32).astype(BF16)
        for n in range(4):
            ps[slot, 0, m, n] = out[64 * n:64 * n + 64, :W]
            ps[slot, 1, n, m] = out[64 * n:64 * n + 64, W:]

    def stage0(k):
        rhs = weights(k)
        for m in range(4):
            rows(lax.rem(k, SL), m, rhs)
        send0(k)

    def send0(k):
        slot = lax.rem(k, SL)
        for t in range(2):
            f = first[t]
            r, l, o = up(f), down(f), opp(f)
            lo, hi = pl.ds(0, 2), pl.ds(2, 2)
            start(k, t, 0, ps.at[slot, t, o, lo], r1.at[slot, t, 0], dev_first(t, r))
            start(k, t, 1, ps.at[slot, t, o, hi], r1.at[slot, t, 1], dev_first(t, l))
            start(k, t, 2, ps.at[slot, t, r, hi], r2.at[slot, t, 0, hi], dev_first(t, r))
            start(k, t, 3, ps.at[slot, t, l, lo], r2.at[slot, t, 1, lo], dev_first(t, l))

    def stage1(k):
        slot = lax.rem(k, SL)
        for t in range(2):
            f = first[t]
            r, l = up(f), down(f)
            lo, hi = pl.ds(0, 2), pl.ds(2, 2)
            arrived(k, t, 0, r1.at[slot, t, 0])
            ps[slot, t, r, lo] = add2(ps[slot, t, r, lo], r1[slot, t, 0])
            start(k, t, 4, ps.at[slot, t, r, lo], r2.at[slot, t, 0, lo], dev_first(t, r))
            arrived(k, t, 1, r1.at[slot, t, 1])
            ps[slot, t, l, hi] = add2(ps[slot, t, l, hi], r1[slot, t, 1])
            start(k, t, 5, ps.at[slot, t, l, hi], r2.at[slot, t, 1, hi], dev_first(t, l))

    def stage2(k):
        slot = lax.rem(k, SL)
        for t in range(2):
            f, s = first[t], second[t]
            lo, hi = pl.ds(0, 2), pl.ds(2, 2)
            arrived(k, t, 2, r2.at[slot, t, 0, hi])
            arrived(k, t, 3, r2.at[slot, t, 1, lo])
            arrived(k, t, 4, r2.at[slot, t, 0, lo])
            arrived(k, t, 5, r2.at[slot, t, 1, hi])
            qs[slot, t] = (
                ps[slot, t, f].astype(F32) + r2[slot, t, 0].astype(F32) + r2[slot, t, 1].astype(F32)
            ).astype(BF16)
            for n in range(6):
                sent(k, t, n, r1.at[slot, t, 0])
            r, l, o = up(s), down(s), opp(s)
            lo, hi = pl.ds(0, 32), pl.ds(32, 32)
            start(k, t, 6, qs.at[slot, t, o, lo], t1.at[slot, t, 0], dev_second(t, r))
            start(k, t, 7, qs.at[slot, t, o, hi], t1.at[slot, t, 1], dev_second(t, l))
            start(k, t, 8, qs.at[slot, t, r, hi], t2.at[slot, t, 0, hi], dev_second(t, r))
            start(k, t, 9, qs.at[slot, t, l, lo], t2.at[slot, t, 1, lo], dev_second(t, l))

    def stage3(k):
        slot = lax.rem(k, SL)
        for t in range(2):
            s = second[t]
            r, l = up(s), down(s)
            lo, hi = pl.ds(0, 32), pl.ds(32, 32)
            arrived(k, t, 6, t1.at[slot, t, 0])
            qs[slot, t, r, lo] = add2(qs[slot, t, r, lo], t1[slot, t, 0])
            start(k, t, 10, qs.at[slot, t, r, lo], t2.at[slot, t, 0, lo], dev_second(t, r))
            arrived(k, t, 7, t1.at[slot, t, 1])
            qs[slot, t, l, hi] = add2(qs[slot, t, l, hi], t1[slot, t, 1])
            start(k, t, 11, qs.at[slot, t, l, hi], t2.at[slot, t, 1, hi], dev_second(t, l))

    def stage4(k):
        slot = lax.rem(k, SL)
        for t in range(2):
            f, s = first[t], second[t]
            lo, hi = pl.ds(0, 32), pl.ds(32, 32)
            arrived(k, t, 8, t2.at[slot, t, 0, hi])
            arrived(k, t, 9, t2.at[slot, t, 1, lo])
            arrived(k, t, 10, t2.at[slot, t, 0, lo])
            arrived(k, t, 11, t2.at[slot, t, 1, hi])
            pre = qs[slot, t, s].astype(F32) + t2[slot, t, 0].astype(F32) + t2[slot, t, 1].astype(F32)
            cdf = 0.5 * (1.0 + lax.erf(pre * INV_ROOT_TWO))
            cols = pl.ds(pl.multiple_of((2 * k + t) * W, W), W)
            @pl.when(k >= SL)
            def _():
                pltpu.make_async_copy(act.at[slot, t], act_hbm.at[:, cols], osem.at[slot, t]).wait()

            act[slot, t] = (pre * cdf).astype(BF16)
            pltpu.make_async_copy(act.at[slot, t], act_hbm.at[:, cols], osem.at[slot, t]).start()
            slope = cdf + pre * jnp.exp(-0.5 * pre * pre) * INV_ROOT_TAU
            gs[k, t, f, s] = (gact[:, cols].astype(F32) * slope).astype(BF16)
            for n in range(6, 12):
                sent(k, t, n, t1.at[slot, t, 0])
            start(k, t, 12, gs.at[k, t, f, s], gs.at[k, t, f, s], dev_second(t, up(s)))
            start(k, t, 13, gs.at[k, t, f, s], gs.at[k, t, f, s], dev_second(t, down(s)))

    def stage5(k):
        for t in range(2):
            f, s = first[t], second[t]
            r, l = up(s), down(s)
            lo, hi = pl.ds(0, 32), pl.ds(32, 32)
            arrived(k, t, 12, gs.at[k, t, f, l])
            start(k, t, 14, gs.at[k, t, f, l, lo], gs.at[k, t, f, l, lo], dev_second(t, r))
            arrived(k, t, 13, gs.at[k, t, f, r])
            start(k, t, 15, gs.at[k, t, f, r, hi], gs.at[k, t, f, r, hi], dev_second(t, l))

    def stage6(k):
        for t in range(2):
            f, s = first[t], second[t]
            o = opp(s)
            lo, hi = pl.ds(0, 32), pl.ds(32, 32)
            arrived(k, t, 14, gs.at[k, t, f, o, lo])
            arrived(k, t, 15, gs.at[k, t, f, o, hi])
            start(k, t, 16, gs.at[k, t, f], gs.at[k, t, f], dev_first(t, up(f)))
            start(k, t, 17, gs.at[k, t, f], gs.at[k, t, f], dev_first(t, down(f)))

    def stage7(k):
        for t in range(2):
            f = first[t]
            r, l = up(f), down(f)
            lo, hi = pl.ds(0, 2), pl.ds(2, 2)
            arrived(k, t, 16, gs.at[k, t, l])
            start(k, t, 18, gs.at[k, t, l, lo], gs.at[k, t, l, lo], dev_first(t, r))
            arrived(k, t, 17, gs.at[k, t, r])
            start(k, t, 19, gs.at[k, t, r, hi], gs.at[k, t, r, hi], dev_first(t, l))

    def gw_copies(k):
        g = lax.rem(k, 2)
        return [
            pltpu.make_async_copy(
                gwst.at[g, r], gw_hbm.at[pl.ds(r * CBK + 2 * WB * k, 2 * WB)], gsem.at[g, r]
            )
            for r in range(RB)
        ]

    def arrive8(k):
        for t in range(2):
            f, s = first[t], second[t]
            o = opp(f)
            lo, hi = pl.ds(0, 2), pl.ds(2, 2)
            arrived(k, t, 18, gs.at[k, t, o, lo])
            arrived(k, t, 19, gs.at[k, t, o, hi])
            sent(k, t, 12, gs.at[k, t, f, s])
            sent(k, t, 13, gs.at[k, t, f, s])
            sent(k, t, 14, gs.at[k, t, f, s, pl.ds(0, 32)])
            sent(k, t, 15, gs.at[k, t, f, s, pl.ds(0, 32)])
            sent(k, t, 16, gs.at[k, t, f])
            sent(k, t, 17, gs.at[k, t, f])
            sent(k, t, 18, gs.at[k, t, o, lo])
            sent(k, t, 19, gs.at[k, t, o, hi])

    def whole_g(k):
        g0 = jnp.concatenate([gs[k, 0, n // 4, n % 4] for n in range(16)], axis=0)
        g1 = jnp.concatenate([gs[k, 1, n % 4, n // 4] for n in range(16)], axis=0)
        return jnp.concatenate([g0, g1], axis=1)

    def slot_grads(k, g):
        @pl.when(k >= 2)
        def _():
            for d in gw_copies(k - 2):
                d.wait()

        wg = jnp.dot(xt[...], g, preferred_element_type=F32).astype(BF16)
        for r in range(RB):
            for j in range(2 * WB):
                gwst[lax.rem(k, 2), r, j] = wg[r * BLK:(r + 1) * BLK, j * BLK:(j + 1) * BLK]
        for d in gw_copies(k):
            d.start()

    def stage8(k):
        arrive8(k)
        g = whole_g(k)
        term = lax.dot_general(
            g, weights(k), (((1,), (1,)), ((), ())), preferred_element_type=F32
        )
        dxa[...] += term.reshape(8, BLK, RB * BLK)
        slot_grads(k, g)

    stages = (stage0, stage1, stage2, stage3, stage4, stage5, stage6, stage7, stage8)

    rhs = weights(0)
    rows(0, z, rhs)
    got(2, xh(zl, c, 1))
    go(9, xh(zl, c, 1), xh(zl, c, 1), sib)
    got(3, xh(zr, c, 0))
    go(10, xh(zr, c, 0), xh(zr, c, 0), sib)
    got(7, xh(zl, 1 - c, 0))
    got(9, xh(zl, 1 - c, 1))
    rows(0, zl, rhs)
    got(8, xh(zr, 1 - c, 1))
    got(10, xh(zr, 1 - c, 0))
    rows(0, zr, rhs)
    got(5, xh(zo, c, 0))
    go(11, xh(zo, c, 0), xh(zo, c, 0), sib)
    got(6, xh(zo, c, 1))
    go(12, xh(zo, c, 1), xh(zo, c, 1), sib)
    got(11, xh(zo, 1 - c, 0))
    got(12, xh(zo, 1 - c, 1))
    rows(0, zo, rhs)
    send0(0)
    for d in sends:
        d.wait_send()
    sends.clear()
    gcopy.wait()
    for r in range(RB):
        for q in range(8):
            xt[r * BLK:(r + 1) * BLK, q * BLK:(q + 1) * BLK] = xs[q, :, r * BLK:(r + 1) * BLK].T

    def body(i, carry):
        for n in range(len(stages) - 1, -1, -1):
            k = i - n

            @pl.when((k >= (0 if n else 1)) & (k < NCH))
            def _():
                stages[n](k)

        return carry

    lax.fori_loop(1, NCH + len(stages) - 2, body, 0)

    last = NCH - 1
    arrive8(last)
    rhs = weights(last)
    for n, q in enumerate((zo, zr, zl, z)):
        g0 = jnp.concatenate([gs[last, 0, q, m] for m in range(4)], axis=0)
        g1 = jnp.concatenate([gs[last, 1, m, q] for m in range(4)], axis=0)
        g = jnp.concatenate([g0, g1], axis=1)
        term = lax.dot_general(g, rhs, (((1,), (1,)), ((), ())), preferred_element_type=F32)
        dxa[pl.ds(2 * q, 2)] += term.reshape(2, BLK, RB * BLK)
        sb[q] = dxa[2 * q + (1 - c)].astype(BF16)
        go(13 + n, sb.at[q], sr.at[q], sib)
    lo, hi = pl.ds(0, 64), pl.ds(64, 64)

    def join(n, q):
        got(13 + n, sr.at[q])
        eb[q] = (dxa[2 * q + c] + sr[q].astype(F32)).astype(BF16)

    join(0, zo)
    go(17, eb.at[zo, lo], u1.at[0], zr_dev)
    go(18, eb.at[zo, hi], u1.at[1], zl_dev)
    join(1, zr)
    go(19, eb.at[zr, hi], u2.at[0, hi], zr_dev)
    join(2, zl)
    go(20, eb.at[zl, lo], u2.at[1, lo], zl_dev)
    join(3, z)
    got(17, u1.at[0])
    eb[zr, lo] = add2(eb[zr, lo], u1[0])
    go(21, eb.at[zr, lo], u2.at[0, lo], zr_dev)
    got(18, u1.at[1])
    eb[zl, hi] = add2(eb[zl, hi], u1[1])
    go(22, eb.at[zl, hi], u2.at[1, hi], zl_dev)
    slot_grads(last, whole_g(last))
    for k in range(NCH - SL, NCH):
        for t in range(2):
            cols = pl.ds((2 * k + t) * W, W)
            pltpu.make_async_copy(
                act.at[k % SL, t], act_hbm.at[:, cols], osem.at[k % SL, t]
            ).wait()
    for k in (last - 1, last):
        for d in gw_copies(k):
            d.wait()
    got(19, u2.at[0, hi])
    got(20, u2.at[1, lo])
    got(21, u2.at[0, lo])
    got(22, u2.at[1, hi])
    dx_out[...] = eb[z].astype(F32) + u2[0].astype(F32) + u2[1].astype(F32)
    for d in sends:
        d.wait_send()


def table_kernel(rows, cols, count, idx):
    row0 = lax.axis_index("inb") * RB
    col0 = lax.axis_index("outb") * CBK

    def clear(n, carry):
        idx[n] = CAP
        return carry

    lax.fori_loop(0, RB * CBK, clear, 0, unroll=8)

    def put(s, carry):
        idx[(rows[s] - row0) * CBK + cols[s] - col0] = s
        return carry

    lax.fori_loop(0, count[0, 0], put, 0)


def pick_kernel(rows, cols, count, act_in, dx_in, gwd, act, dx, gw, abuf, dbuf, gbuf, obuf, sem, gsem, osem):
    row0 = lax.axis_index("inb") * RB
    col0 = lax.axis_index("outb") * CBK

    def fetch(s):
        cell = (rows[s] - row0) * CBK + cols[s] - col0
        return pltpu.make_async_copy(gwd.at[cell], gbuf.at[s], gsem.at[s])

    def begin(s, carry):
        fetch(s).start()
        return carry

    lax.fori_loop(0, CAP, begin, 0, unroll=4)
    ins = [
        pltpu.make_async_copy(act_in, abuf, sem.at[0]),
        pltpu.make_async_copy(dx_in, dbuf, sem.at[1]),
    ]
    for d in ins:
        d.start()
    outs = [
        pltpu.make_async_copy(abuf, act, sem.at[2]),
        pltpu.make_async_copy(dbuf, dx, sem.at[3]),
    ]

    def flush(n):
        return pltpu.make_async_copy(
            obuf.at[pl.ds(n * 8, 8)], gw.at[pl.ds(n * 8, 8)], osem.at[n]
        )

    def group(n, carry):
        for m in range(8):
            s = n * 8 + m
            fetch(s).wait()
            alive = (s < count[0, 0]).astype(F32)
            obuf[s] = gbuf[s].astype(F32) * alive
        flush(n).start()
        return carry

    lax.fori_loop(0, CAP // 8, group, 0)
    for d, e in zip(ins, outs):
        d.wait()
        e.start()

    def done(n, carry):
        flush(n).wait()
        return carry

    lax.fori_loop(0, CAP // 8, done, 0)
    for e in outs:
        e.wait()


def per_device(tokens, weight_blocks, block_rows, block_cols, block_count, grad_act):
    vmem = pl.BlockSpec(memory_space=pltpu.VMEM)
    smem = pl.BlockSpec(memory_space=pltpu.SMEM)
    hbm = pl.BlockSpec(memory_space=pl.ANY)
    rows, cols, count = block_rows[0, 0], block_cols[0, 0], block_count
    act_shape = jax.ShapeDtypeStruct((64, CBK * BLK), BF16)
    dx_shape = jax.ShapeDtypeStruct((BLK, RB * BLK), F32)
    idx = pl.pallas_call(
        table_kernel,
        out_shape=jax.ShapeDtypeStruct((RB * CBK,), jnp.int32),
        in_specs=[smem, smem, smem],
        out_specs=smem,
        name="table",
    )(rows, cols, count)
    act, dx, gwd = pl.pallas_call(
        kernel,
        out_shape=(
            act_shape,
            dx_shape,
            jax.ShapeDtypeStruct((RB * CBK, BLK, BLK), BF16),
        ),
        in_specs=[smem, hbm, hbm, hbm],
        out_specs=(hbm, vmem, hbm),
        scratch_shapes=[
            pltpu.VMEM((CAP + 1, BLK, BLK), BF16),
            pltpu.VMEM((8, BLK, RB * BLK), BF16),
            pltpu.VMEM((RB * BLK, 1024), BF16),
            pltpu.VMEM((SL, 2, 4, 4, 64, W), BF16),
            pltpu.VMEM((SL, 2, 2, 2, 64, W), BF16),
            pltpu.VMEM((SL, 2, 2, 4, 64, W), BF16),
            pltpu.VMEM((SL, 2, 4, 64, W), BF16),
            pltpu.VMEM((SL, 2, 2, 32, W), BF16),
            pltpu.VMEM((SL, 2, 2, 64, W), BF16),
            pltpu.VMEM((NCH, 2, 4, 4, 64, W), BF16),
            pltpu.VMEM((8, BLK, RB * BLK), F32),
            pltpu.VMEM((64, CBK * BLK), BF16),
            pltpu.VMEM((SL, 2, 64, W), BF16),
            pltpu.VMEM((2, RB, 2 * WB, BLK, BLK), BF16),
            pltpu.VMEM((4, BLK, RB * BLK), BF16),
            pltpu.VMEM((4, BLK, RB * BLK), BF16),
            pltpu.VMEM((4, BLK, RB * BLK), BF16),
            pltpu.VMEM((2, 64, RB * BLK), BF16),
            pltpu.VMEM((2, BLK, RB * BLK), BF16),
            pltpu.SemaphoreType.DMA((SL, 2, 20)),
            pltpu.SemaphoreType.DMA((SL, 2, 20)),
            pltpu.SemaphoreType.DMA((23,)),
            pltpu.SemaphoreType.DMA((23,)),
            pltpu.SemaphoreType.DMA((3,)),
            pltpu.SemaphoreType.DMA((SL, 2)),
            pltpu.SemaphoreType.DMA((2, RB)),
        ],
        compiler_params=pltpu.CompilerParams(
            collective_id=0, has_side_effects=True, vmem_limit_bytes=67043328
        ),
        name="ffn",
    )(idx, tokens, weight_blocks[0, 0], grad_act)
    act, dx, gw = pl.pallas_call(
        pick_kernel,
        out_shape=(act_shape, dx_shape, jax.ShapeDtypeStruct((CAP, BLK, BLK), F32)),
        in_specs=[smem, smem, smem, hbm, hbm, hbm],
        out_specs=(hbm, hbm, hbm),
        scratch_shapes=[
            pltpu.VMEM(act_shape.shape, BF16),
            pltpu.VMEM(dx_shape.shape, F32),
            pltpu.VMEM((CAP, BLK, BLK), BF16),
            pltpu.VMEM((CAP, BLK, BLK), F32),
            pltpu.SemaphoreType.DMA((4,)),
            pltpu.SemaphoreType.DMA((CAP,)),
            pltpu.SemaphoreType.DMA((CAP // 8,)),
        ],
        compiler_params=pltpu.CompilerParams(vmem_limit_bytes=67043328),
        name="pick",
    )(rows, cols, count, act, dx, gwd)
    return (act, dx, gw[None, None])


def solution(mesh):
    in_specs = (
        P("outb", "inb"),
        P("inb", "outb", None, None, None),
        P("inb", "outb", None),
        P("inb", "outb", None),
        P("inb", "outb"),
        P("inb", "outb"),
    )
    out_specs = (P("inb", "outb"), P("outb", "inb"), P("inb", "outb", None, None, None))
    return jax.shard_map(
        per_device, mesh=mesh, in_specs=in_specs, out_specs=out_specs, check_vma=False
    )
```

```python
import functools

import jax
import jax.numpy as jnp
from jax import lax
from jax.experimental import pallas as pl
from jax.experimental.pallas import tpu as pltpu
from jax.sharding import PartitionSpec as P

MESH = pl.DeviceIdType.MESH
F32 = jnp.float32
BF16 = jnp.bfloat16
INV_ROOT_TWO = 0.7071067811865476
INV_ROOT_TAU = 0.3989422804014327
BLK = 128
RB = 6
CBK = 48
CAP = 72
WB = 3
W = WB * BLK
NCH = CBK // (2 * WB)
SL = 4


def add2(a, b):
    return (a.astype(F32) + b.astype(F32)).astype(BF16)


def kernel(
    rows_in, cols_in, count_in, tok, wblk, gact_hbm,
    act_hbm, dx_out, gw_hbm,
    idx, tbl,
    wp, xs, xt, ps, r1, r2, qs, t1, t2, gs, dxa, gact, act, gwst, sb, sr, eb, u1, u2,
    ssem, rsem, asem, arsem, lsem, osem, gsem,
):
    a = lax.axis_index("inb")
    b = lax.axis_index("outb")
    x, y = a // 4, a % 4
    z, c = b // 2, b % 2

    def up(v):
        return lax.rem(v + 1, 4)

    def down(v):
        return lax.rem(v + 3, 4)

    def opp(v):
        return lax.rem(v + 2, 4)

    zr, zl, zo = up(z), down(z), opp(z)
    sib = (a, 2 * z + (1 - c))
    zr_dev, zl_dev = (a, 2 * zr + c), (a, 2 * zl + c)

    first = (x, y)
    second = (y, x)

    def dev_first(t, v):
        return (4 * v + y, b) if t == 0 else (4 * x + v, b)

    def dev_second(t, v):
        return (4 * x + v, b) if t == 0 else (4 * v + y, b)

    wcopy = pltpu.make_async_copy(wblk, wp.at[pl.ds(0, CAP)], lsem.at[0])
    wcopy.start()
    xcopy = pltpu.make_async_copy(tok, xs.at[b], lsem.at[1])
    xcopy.start()
    gcopy = pltpu.make_async_copy(gact_hbm, gact, lsem.at[2])
    gcopy.start()

    barrier = pltpu.get_barrier_semaphore()
    for dev in (
        dev_first(0, up(x)), dev_first(0, down(x)),
        dev_first(1, up(y)), dev_first(1, down(y)),
        zr_dev, zl_dev, sib,
    ):
        pl.semaphore_signal(barrier, inc=1, device_id=dev, device_id_type=MESH)
    wp[CAP] = jnp.zeros((BLK, BLK), BF16)

    flat = BLK * lax.broadcasted_iota(jnp.int32, (8, BLK), 0) + lax.broadcasted_iota(jnp.int32, (8, BLK), 1)

    def place(n, found):
        cell = (rows_in[n] - a * RB) * CBK + cols_in[n] - b * CBK
        cell = jnp.where(n < count_in[0, 0], cell, 8 * BLK)
        return jnp.where(flat == cell, n, found)

    tbl[...] = lax.fori_loop(0, CAP, place, jnp.full((8, BLK), CAP, jnp.int32), unroll=4)
    tcopy = pltpu.make_async_copy(tbl, idx, lsem.at[3])
    tcopy.start()
    pl.semaphore_wait(barrier, 7)

    def ac(n, src, dst, dev):
        return pltpu.make_async_remote_copy(
            src_ref=src, dst_ref=dst, send_sem=asem.at[n], recv_sem=arsem.at[n],
            device_id=dev, device_id_type=MESH,
        )

    def xb(zz, cc):
        return xs.at[2 * zz + cc]

    def xq(zz, cc, h):
        return xs.at[2 * zz + cc, pl.ds(32 * h, 32)]

    sends = []

    def go(n, src, dst, dev):
        d = ac(n, src, dst, dev)
        d.start()
        sends.append(d)

    def got(n, dst):
        ac(n, dst, dst, sib).wait_recv()

    for n in range(4):
        m = (n + 2) % 4
        go(n, tok.at[pl.ds(32 * n, 32)], xq(z, c, n), zr_dev)
        go(4 + n, tok.at[pl.ds(32 * m, 32)], xq(z, c, m), zl_dev)
    go(8, tok, xb(z, c), sib)
    dxa[...] = jnp.zeros_like(dxa)
    for n in range(2):
        got(n, xq(zl, c, n))
        go(9 + n, xq(zl, c, n), xq(zl, c, n), zr_dev)
        got(4 + n, xq(zr, c, n + 2))
        go(11 + n, xq(zr, c, n + 2), xq(zr, c, n + 2), zl_dev)
        go(13 + n, xq(zl, c, n), xq(zl, c, n), sib)
        go(15 + n, xq(zr, c, n + 2), xq(zr, c, n + 2), sib)
    xcopy.wait()
    wcopy.wait()
    tcopy.wait()
    got(8, xb(z, 1 - c))

    def weights(k):
        cols = []
        for j in range(2 * WB):
            col = 2 * WB * k + j
            cols.append(jnp.concatenate([wp[idx[(r * CBK + col) // BLK, (r * CBK + col) % BLK]] for r in range(RB)], axis=0))
        return jnp.concatenate(cols, axis=1)

    def copy(k, t, n, src, dst, dev):
        slot = lax.rem(k, SL)
        return pltpu.make_async_remote_copy(
            src_ref=src, dst_ref=dst,
            send_sem=ssem.at[slot, t, n], recv_sem=rsem.at[slot, t, n],
            device_id=dev, device_id_type=MESH,
        )

    def start(k, t, n, src, dst, dev):
        copy(k, t, n, src, dst, dev).start()

    def arrived(k, t, n, dst):
        copy(k, t, n, dst, dst, sib).wait_recv()

    def sent(k, t, n, src):
        copy(k, t, n, src, src, sib).wait_send()

    def rows(slot, m, rhs):
        lhs = jnp.concatenate([xs[2 * m], xs[2 * m + 1]], axis=0)
        out = jnp.dot(lhs, rhs, preferred_element_type=F32).astype(BF16)
        for n in range(4):
            ps[slot, 0, m, n] = out[64 * n:64 * n + 64, :W]
            ps[slot, 1, n, m] = out[64 * n:64 * n + 64, W:]

    def stage0(k):
        rhs = weights(k)
        for m in range(4):
            rows(lax.rem(k, SL), m, rhs)
        send0(k)

    def send0(k):
        slot = lax.rem(k, SL)
        for t in range(2):
            f = first[t]
            r, l, o = up(f), down(f), opp(f)
            lo, hi = pl.ds(0, 2), pl.ds(2, 2)
            start(k, t, 0, ps.at[slot, t, o, lo], r1.at[slot, t, 0], dev_first(t, r))
            start(k, t, 1, ps.at[slot, t, o, hi], r1.at[slot, t, 1], dev_first(t, l))
            start(k, t, 2, ps.at[slot, t, r, hi], r2.at[slot, t, 0, hi], dev_first(t, r))
            start(k, t, 3, ps.at[slot, t, l, lo], r2.at[slot, t, 1, lo], dev_first(t, l))

    def stage1(k):
        slot = lax.rem(k, SL)
        for t in range(2):
            f = first[t]
            r, l = up(f), down(f)
            lo, hi = pl.ds(0, 2), pl.ds(2, 2)
            arrived(k, t, 0, r1.at[slot, t, 0])
            ps[slot, t, r, lo] = add2(ps[slot, t, r, lo], r1[slot, t, 0])
            start(k, t, 4, ps.at[slot, t, r, lo], r2.at[slot, t, 0, lo], dev_first(t, r))
            arrived(k, t, 1, r1.at[slot, t, 1])
            ps[slot, t, l, hi] = add2(ps[slot, t, l, hi], r1[slot, t, 1])
            start(k, t, 5, ps.at[slot, t, l, hi], r2.at[slot, t, 1, hi], dev_first(t, l))

    def stage2(k):
        slot = lax.rem(k, SL)
        for t in range(2):
            f, s = first[t], second[t]
            lo, hi = pl.ds(0, 2), pl.ds(2, 2)
            arrived(k, t, 2, r2.at[slot, t, 0, hi])
            arrived(k, t, 3, r2.at[slot, t, 1, lo])
            arrived(k, t, 4, r2.at[slot, t, 0, lo])
            arrived(k, t, 5, r2.at[slot, t, 1, hi])
            qs[slot, t] = (
                ps[slot, t, f].astype(F32) + r2[slot, t, 0].astype(F32) + r2[slot, t, 1].astype(F32)
            ).astype(BF16)
            for n in range(6):
                sent(k, t, n, r1.at[slot, t, 0])
            r, l, o = up(s), down(s), opp(s)
            lo, hi = pl.ds(0, 32), pl.ds(32, 32)
            start(k, t, 6, qs.at[slot, t, o, lo], t1.at[slot, t, 0], dev_second(t, r))
            start(k, t, 7, qs.at[slot, t, o, hi], t1.at[slot, t, 1], dev_second(t, l))
            start(k, t, 8, qs.at[slot, t, r, hi], t2.at[slot, t, 0, hi], dev_second(t, r))
            start(k, t, 9, qs.at[slot, t, l, lo], t2.at[slot, t, 1, lo], dev_second(t, l))

    def stage3(k):
        slot = lax.rem(k, SL)
        for t in range(2):
            s = second[t]
            r, l = up(s), down(s)
            lo, hi = pl.ds(0, 32), pl.ds(32, 32)
            arrived(k, t, 6, t1.at[slot, t, 0])
            qs[slot, t, r, lo] = add2(qs[slot, t, r, lo], t1[slot, t, 0])
            start(k, t, 10, qs.at[slot, t, r, lo], t2.at[slot, t, 0, lo], dev_second(t, r))
            arrived(k, t, 7, t1.at[slot, t, 1])
            qs[slot, t, l, hi] = add2(qs[slot, t, l, hi], t1[slot, t, 1])
            start(k, t, 11, qs.at[slot, t, l, hi], t2.at[slot, t, 1, hi], dev_second(t, l))

    def stage4(k):
        slot = lax.rem(k, SL)
        for t in range(2):
            f, s = first[t], second[t]
            lo, hi = pl.ds(0, 32), pl.ds(32, 32)
            arrived(k, t, 8, t2.at[slot, t, 0, hi])
            arrived(k, t, 9, t2.at[slot, t, 1, lo])
            arrived(k, t, 10, t2.at[slot, t, 0, lo])
            arrived(k, t, 11, t2.at[slot, t, 1, hi])
            pre = qs[slot, t, s].astype(F32) + t2[slot, t, 0].astype(F32) + t2[slot, t, 1].astype(F32)
            cdf = 0.5 * (1.0 + lax.erf(pre * INV_ROOT_TWO))
            cols = pl.ds(pl.multiple_of((2 * k + t) * W, W), W)
            @pl.when(k >= SL)
            def _():
                pltpu.make_async_copy(act.at[slot, t], act_hbm.at[:, cols], osem.at[slot, t]).wait()

            act[slot, t] = (pre * cdf).astype(BF16)
            pltpu.make_async_copy(act.at[slot, t], act_hbm.at[:, cols], osem.at[slot, t]).start()
            slope = cdf + pre * jnp.exp(-0.5 * pre * pre) * INV_ROOT_TAU
            gs[k, t, f, s] = (gact[:, cols].astype(F32) * slope).astype(BF16)
            for n in range(6, 12):
                sent(k, t, n, t1.at[slot, t, 0])
            start(k, t, 12, gs.at[k, t, f, s], gs.at[k, t, f, s], dev_second(t, up(s)))
            start(k, t, 13, gs.at[k, t, f, s], gs.at[k, t, f, s], dev_second(t, down(s)))

    def stage5(k):
        for t in range(2):
            f, s = first[t], second[t]
            r, l = up(s), down(s)
            lo, hi = pl.ds(0, 32), pl.ds(32, 32)
            arrived(k, t, 12, gs.at[k, t, f, l])
            start(k, t, 14, gs.at[k, t, f, l, lo], gs.at[k, t, f, l, lo], dev_second(t, r))
            arrived(k, t, 13, gs.at[k, t, f, r])
            start(k, t, 15, gs.at[k, t, f, r, hi], gs.at[k, t, f, r, hi], dev_second(t, l))

    def stage6(k):
        for t in range(2):
            f, s = first[t], second[t]
            o = opp(s)
            lo, hi = pl.ds(0, 32), pl.ds(32, 32)
            arrived(k, t, 14, gs.at[k, t, f, o, lo])
            arrived(k, t, 15, gs.at[k, t, f, o, hi])
            start(k, t, 16, gs.at[k, t, f], gs.at[k, t, f], dev_first(t, up(f)))
            start(k, t, 17, gs.at[k, t, f], gs.at[k, t, f], dev_first(t, down(f)))

    def stage7(k):
        for t in range(2):
            f = first[t]
            r, l = up(f), down(f)
            lo, hi = pl.ds(0, 2), pl.ds(2, 2)
            arrived(k, t, 16, gs.at[k, t, l])
            start(k, t, 18, gs.at[k, t, l, lo], gs.at[k, t, l, lo], dev_first(t, r))
            arrived(k, t, 17, gs.at[k, t, r])
            start(k, t, 19, gs.at[k, t, r, hi], gs.at[k, t, r, hi], dev_first(t, l))

    def gw_copies(k):
        g = lax.rem(k, 2)
        return [
            pltpu.make_async_copy(
                gwst.at[g, r], gw_hbm.at[pl.ds(r * CBK + 2 * WB * k, 2 * WB)], gsem.at[g, r]
            )
            for r in range(RB)
        ]

    def arrive8(k):
        for t in range(2):
            f, s = first[t], second[t]
            o = opp(f)
            lo, hi = pl.ds(0, 2), pl.ds(2, 2)
            arrived(k, t, 18, gs.at[k, t, o, lo])
            arrived(k, t, 19, gs.at[k, t, o, hi])
            sent(k, t, 12, gs.at[k, t, f, s])
            sent(k, t, 13, gs.at[k, t, f, s])
            sent(k, t, 14, gs.at[k, t, f, s, pl.ds(0, 32)])
            sent(k, t, 15, gs.at[k, t, f, s, pl.ds(0, 32)])
            sent(k, t, 16, gs.at[k, t, f])
            sent(k, t, 17, gs.at[k, t, f])
            sent(k, t, 18, gs.at[k, t, o, lo])
            sent(k, t, 19, gs.at[k, t, o, hi])

    def whole_g(k):
        g0 = jnp.concatenate([gs[k, 0, n // 4, n % 4] for n in range(16)], axis=0)
        g1 = jnp.concatenate([gs[k, 1, n % 4, n // 4] for n in range(16)], axis=0)
        return jnp.concatenate([g0, g1], axis=1)

    def slot_grads(k, g):
        @pl.when(k >= 2)
        def _():
            for d in gw_copies(k - 2):
                d.wait()

        wg = jnp.dot(xt[...], g, preferred_element_type=F32).astype(BF16)
        for r in range(RB):
            for j in range(2 * WB):
                gwst[lax.rem(k, 2), r, j] = wg[r * BLK:(r + 1) * BLK, j * BLK:(j + 1) * BLK]
        for d in gw_copies(k):
            d.start()

    def stage8(k):
        arrive8(k)
        g = whole_g(k)
        term = lax.dot_general(
            g, weights(k), (((1,), (1,)), ((), ())), preferred_element_type=F32
        )
        dxa[...] += term.reshape(8, BLK, RB * BLK)
        slot_grads(k, g)

    stages = (stage0, stage1, stage2, stage3, stage4, stage5, stage6, stage7, stage8)

    rhs = weights(0)
    rows(0, z, rhs)
    for n in range(2):
        got(2 + n, xq(zl, c, n + 2))
        go(17 + n, xq(zl, c, n + 2), xq(zl, c, n + 2), sib)
        got(6 + n, xq(zr, c, n))
        go(19 + n, xq(zr, c, n), xq(zr, c, n), sib)
    for n in range(2):
        got(9 + n, xq(zo, c, n))
        go(21 + n, xq(zo, c, n), xq(zo, c, n), sib)
        got(11 + n, xq(zo, c, n + 2))
        go(23 + n, xq(zo, c, n + 2), xq(zo, c, n + 2), sib)
    for n in range(2):
        got(13 + n, xq(zl, 1 - c, n))
        got(17 + n, xq(zl, 1 - c, n + 2))
    rows(0, zl, rhs)
    for n in range(2):
        got(15 + n, xq(zr, 1 - c, n + 2))
        got(19 + n, xq(zr, 1 - c, n))
    rows(0, zr, rhs)
    for n in range(2):
        got(21 + n, xq(zo, 1 - c, n))
        got(23 + n, xq(zo, 1 - c, n + 2))
    rows(0, zo, rhs)
    send0(0)
    for d in sends:
        d.wait_send()
    sends.clear()
    gcopy.wait()

    def body(i, carry):
        @pl.when(i == 2)
        def _():
            for r in range(RB):
                for q in range(8):
                    xt[r * BLK:(r + 1) * BLK, q * BLK:(q + 1) * BLK] = xs[q, :, r * BLK:(r + 1) * BLK].T

        for n in range(len(stages) - 1, -1, -1):
            k = i - n

            @pl.when((k >= (0 if n else 1)) & (k < NCH))
            def _():
                stages[n](k)

        return carry

    lax.fori_loop(1, NCH + len(stages) - 2, body, 0)

    last = NCH - 1
    arrive8(last)
    rhs = weights(last)
    for n, q in enumerate((zo, zr, zl, z)):
        g0 = jnp.concatenate([gs[last, 0, q, m] for m in range(4)], axis=0)
        g1 = jnp.concatenate([gs[last, 1, m, q] for m in range(4)], axis=0)
        g = jnp.concatenate([g0, g1], axis=1)
        term = lax.dot_general(g, rhs, (((1,), (1,)), ((), ())), preferred_element_type=F32)
        dxa[pl.ds(2 * q, 2)] += term.reshape(2, BLK, RB * BLK)
        sb[q] = dxa[2 * q + (1 - c)].astype(BF16)
        go(25 + n, sb.at[q], sr.at[q], sib)
    lo, hi = pl.ds(0, 64), pl.ds(64, 64)

    def join(n, q):
        got(25 + n, sr.at[q])
        eb[q] = (dxa[2 * q + c] + sr[q].astype(F32)).astype(BF16)

    join(0, zo)
    go(29, eb.at[zo, lo], u1.at[0], zr_dev)
    go(30, eb.at[zo, hi], u1.at[1], zl_dev)
    join(1, zr)
    go(31, eb.at[zr, hi], u2.at[0, hi], zr_dev)
    join(2, zl)
    go(32, eb.at[zl, lo], u2.at[1, lo], zl_dev)
    join(3, z)
    got(29, u1.at[0])
    eb[zr, lo] = add2(eb[zr, lo], u1[0])
    go(33, eb.at[zr, lo], u2.at[0, lo], zr_dev)
    got(30, u1.at[1])
    eb[zl, hi] = add2(eb[zl, hi], u1[1])
    go(34, eb.at[zl, hi], u2.at[1, hi], zl_dev)
    slot_grads(last, whole_g(last))
    for k in range(NCH - SL, NCH):
        for t in range(2):
            cols = pl.ds((2 * k + t) * W, W)
            pltpu.make_async_copy(
                act.at[k % SL, t], act_hbm.at[:, cols], osem.at[k % SL, t]
            ).wait()
    for k in (last - 1, last):
        for d in gw_copies(k):
            d.wait()
    got(31, u2.at[0, hi])
    got(32, u2.at[1, lo])
    got(33, u2.at[0, lo])
    got(34, u2.at[1, hi])
    dx_out[...] = eb[z].astype(F32) + u2[0].astype(F32) + u2[1].astype(F32)
    for d in sends:
        d.wait_send()


def pick_kernel(rows, cols, count, act_in, dx_in, gwd, act, dx, gw, abuf, dbuf, gbuf, obuf, sem, gsem, osem):
    row0 = lax.axis_index("inb") * RB
    col0 = lax.axis_index("outb") * CBK

    def fetch(s):
        cell = (rows[s] - row0) * CBK + cols[s] - col0
        return pltpu.make_async_copy(gwd.at[cell], gbuf.at[s], gsem.at[s])

    def begin(s, carry):
        fetch(s).start()
        return carry

    lax.fori_loop(0, CAP, begin, 0, unroll=4)
    ins = [
        pltpu.make_async_copy(act_in, abuf, sem.at[0]),
        pltpu.make_async_copy(dx_in, dbuf, sem.at[1]),
    ]
    for d in ins:
        d.start()
    outs = [
        pltpu.make_async_copy(abuf, act, sem.at[2]),
        pltpu.make_async_copy(dbuf, dx, sem.at[3]),
    ]

    def flush(n):
        return pltpu.make_async_copy(
            obuf.at[pl.ds(n * 8, 8)], gw.at[pl.ds(n * 8, 8)], osem.at[n]
        )

    def group(n, carry):
        for m in range(8):
            s = n * 8 + m
            fetch(s).wait()
            alive = (s < count[0, 0]).astype(F32)
            obuf[s] = gbuf[s].astype(F32) * alive
        flush(n).start()
        return carry

    lax.fori_loop(0, CAP // 8, group, 0)
    for d, e in zip(ins, outs):
        d.wait()
        e.start()

    def done(n, carry):
        flush(n).wait()
        return carry

    lax.fori_loop(0, CAP // 8, done, 0)
    for e in outs:
        e.wait()


def per_device(tokens, weight_blocks, block_rows, block_cols, block_count, grad_act):
    vmem = pl.BlockSpec(memory_space=pltpu.VMEM)
    smem = pl.BlockSpec(memory_space=pltpu.SMEM)
    hbm = pl.BlockSpec(memory_space=pl.ANY)
    rows, cols, count = block_rows[0, 0], block_cols[0, 0], block_count
    act_shape = jax.ShapeDtypeStruct((64, CBK * BLK), BF16)
    dx_shape = jax.ShapeDtypeStruct((BLK, RB * BLK), F32)
    act, dx, gwd = pl.pallas_call(
        kernel,
        out_shape=(
            act_shape,
            dx_shape,
            jax.ShapeDtypeStruct((RB * CBK, BLK, BLK), BF16),
        ),
        in_specs=[smem, smem, smem, hbm, hbm, hbm],
        out_specs=(hbm, vmem, hbm),
        scratch_shapes=[
            pltpu.SMEM((8, BLK), jnp.int32),
            pltpu.VMEM((8, BLK), jnp.int32),
            pltpu.VMEM((CAP + 1, BLK, BLK), BF16),
            pltpu.VMEM((8, BLK, RB * BLK), BF16),
            pltpu.VMEM((RB * BLK, 1024), BF16),
            pltpu.VMEM((SL, 2, 4, 4, 64, W), BF16),
            pltpu.VMEM((SL, 2, 2, 2, 64, W), BF16),
            pltpu.VMEM((SL, 2, 2, 4, 64, W), BF16),
            pltpu.VMEM((SL, 2, 4, 64, W), BF16),
            pltpu.VMEM((SL, 2, 2, 32, W), BF16),
            pltpu.VMEM((SL, 2, 2, 64, W), BF16),
            pltpu.VMEM((NCH, 2, 4, 4, 64, W), BF16),
            pltpu.VMEM((8, BLK, RB * BLK), F32),
            pltpu.VMEM((64, CBK * BLK), BF16),
            pltpu.VMEM((SL, 2, 64, W), BF16),
            pltpu.VMEM((2, RB, 2 * WB, BLK, BLK), BF16),
            pltpu.VMEM((4, BLK, RB * BLK), BF16),
            pltpu.VMEM((4, BLK, RB * BLK), BF16),
            pltpu.VMEM((4, BLK, RB * BLK), BF16),
            pltpu.VMEM((2, 64, RB * BLK), BF16),
            pltpu.VMEM((2, BLK, RB * BLK), BF16),
            pltpu.SemaphoreType.DMA((SL, 2, 20)),
            pltpu.SemaphoreType.DMA((SL, 2, 20)),
            pltpu.SemaphoreType.DMA((35,)),
            pltpu.SemaphoreType.DMA((35,)),
            pltpu.SemaphoreType.DMA((4,)),
            pltpu.SemaphoreType.DMA((SL, 2)),
            pltpu.SemaphoreType.DMA((2, RB)),
        ],
        compiler_params=pltpu.CompilerParams(
            collective_id=0, has_side_effects=True, vmem_limit_bytes=67043328
        ),
        name="ffn",
    )(rows, cols, count, tokens, weight_blocks[0, 0], grad_act)
    act, dx, gw = pl.pallas_call(
        pick_kernel,
        out_shape=(act_shape, dx_shape, jax.ShapeDtypeStruct((CAP, BLK, BLK), F32)),
        in_specs=[smem, smem, smem, hbm, hbm, hbm],
        out_specs=(hbm, hbm, hbm),
        scratch_shapes=[
            pltpu.VMEM(act_shape.shape, BF16),
            pltpu.VMEM(dx_shape.shape, F32),
            pltpu.VMEM((CAP, BLK, BLK), BF16),
            pltpu.VMEM((CAP, BLK, BLK), F32),
            pltpu.SemaphoreType.DMA((4,)),
            pltpu.SemaphoreType.DMA((CAP,)),
            pltpu.SemaphoreType.DMA((CAP // 8,)),
        ],
        compiler_params=pltpu.CompilerParams(vmem_limit_bytes=67043328),
        name="pick",
    )(rows, cols, count, act, dx, gwd)
    return (act, dx, gw[None, None])


def solution(mesh):
    in_specs = (
        P("outb", "inb"),
        P("inb", "outb", None, None, None),
        P("inb", "outb", None),
        P("inb", "outb", None),
        P("inb", "outb"),
        P("inb", "outb"),
    )
    out_specs = (P("inb", "outb"), P("outb", "inb"), P("inb", "outb", None, None, None))
    return jax.shard_map(
        per_device, mesh=mesh, in_specs=in_specs, out_specs=out_specs, check_vma=False
    )
```

```python
import functools

import jax
import jax.numpy as jnp
from jax import lax
from jax.experimental import pallas as pl
from jax.experimental.pallas import tpu as pltpu
from jax.sharding import PartitionSpec as P

MESH = pl.DeviceIdType.MESH
F32 = jnp.float32
BF16 = jnp.bfloat16
INV_ROOT_TWO = 0.7071067811865476
INV_ROOT_TAU = 0.3989422804014327
BLK = 128
RB = 6
CBK = 48
CAP = 72
WB = 3
W = WB * BLK
NCH = CBK // (2 * WB)
SL = 4
EARLY = 1


def add2(a, b):
    return (a.astype(F32) + b.astype(F32)).astype(BF16)


def kernel(
    rows_in, cols_in, count_in, tok, wblk, gact_hbm,
    act_hbm, dx_out, gw_hbm,
    idx, tbl,
    wp, xs, xt, ps, r1, r2, qs, t1, t2, gs, dxa, gact, act, gwst, sb, sr, eb, u1, u2,
    ssem, rsem, asem, arsem, lsem, osem, gsem,
):
    a = lax.axis_index("inb")
    b = lax.axis_index("outb")
    x, y = a // 4, a % 4
    z, c = b // 2, b % 2

    def up(v):
        return lax.rem(v + 1, 4)

    def down(v):
        return lax.rem(v + 3, 4)

    def opp(v):
        return lax.rem(v + 2, 4)

    zr, zl = up(z), down(z)
    sib = (a, 2 * z + (1 - c))
    zr_dev, zl_dev = (a, 2 * zr + c), (a, 2 * zl + c)

    xr = lax.rem(x - z + 5, 4)
    first = (xr, y)
    second = (y, xr)

    def dev_x(v):
        return (4 * lax.rem(v + z + 3, 4) + y, b)

    def dev_y(v):
        return (4 * x + v, b)

    def dev_first(t, v):
        return dev_x(v) if t == 0 else dev_y(v)

    def dev_second(t, v):
        return dev_y(v) if t == 0 else dev_x(v)

    wcopy = pltpu.make_async_copy(wblk, wp.at[pl.ds(0, CAP)], lsem.at[0])
    wcopy.start()
    xcopy = pltpu.make_async_copy(tok, xs.at[2 + c], lsem.at[1])
    xcopy.start()
    gcopy = pltpu.make_async_copy(gact_hbm, gact, lsem.at[2])
    gcopy.start()

    barrier = pltpu.get_barrier_semaphore()
    for dev in (
        dev_x(up(xr)), dev_x(down(xr)), dev_y(up(y)), dev_y(down(y)),
        zr_dev, zl_dev, sib,
    ):
        pl.semaphore_signal(barrier, inc=1, device_id=dev, device_id_type=MESH)
    wp[CAP] = jnp.zeros((BLK, BLK), BF16)

    flat = BLK * lax.broadcasted_iota(jnp.int32, (8, BLK), 0) + lax.broadcasted_iota(jnp.int32, (8, BLK), 1)

    def place(n, found):
        cell = (rows_in[n] - a * RB) * CBK + cols_in[n] - b * CBK
        cell = jnp.where(n < count_in[0, 0], cell, 8 * BLK)
        return jnp.where(flat == cell, n, found)

    tbl[...] = lax.fori_loop(0, CAP, place, jnp.full((8, BLK), CAP, jnp.int32), unroll=4)
    tcopy = pltpu.make_async_copy(tbl, idx, lsem.at[3])
    tcopy.start()
    pl.semaphore_wait(barrier, 7)

    def ac(part, n, src, dst, dev):
        return pltpu.make_async_remote_copy(
            src_ref=src, dst_ref=dst, send_sem=asem.at[part], recv_sem=arsem.at[n],
            device_id=dev, device_id_type=MESH,
        )

    def go(part, n, src, dst, dev):
        ac(part, n, src, dst, dev).start()

    def got(n, dst):
        ac(0, n, dst, dst, sib).wait_recv()

    def xq(j, cc, h):
        return xs.at[2 * j + cc, pl.ds(32 * h, 32)]

    for n in range(4):
        m = (n + 2) % 4
        go(0, n, tok.at[pl.ds(32 * n, 32)], xq(0, c, n), zr_dev)
        go(0, 4 + m, tok.at[pl.ds(32 * m, 32)], xq(2, c, m), zl_dev)
    go(0, 8, tok, xs.at[2 + c], sib)
    dxa[...] = jnp.zeros_like(dxa)
    xcopy.wait()
    wcopy.wait()
    tcopy.wait()
    got(8, xs.at[2 + 1 - c])

    def weights(k):
        cols = []
        for j in range(2 * WB):
            col = 2 * WB * k + j
            cols.append(jnp.concatenate([wp[idx[(r * CBK + col) // BLK, (r * CBK + col) % BLK]] for r in range(RB)], axis=0))
        return jnp.concatenate(cols, axis=1)

    def copy(k, t, part, n, src, dst, dev):
        slot = lax.rem(k, SL)
        return pltpu.make_async_remote_copy(
            src_ref=src, dst_ref=dst,
            send_sem=ssem.at[slot, t, part], recv_sem=rsem.at[slot, t, n],
            device_id=dev, device_id_type=MESH,
        )

    def start(k, t, n, src, dst, dev):
        copy(k, t, n // 3, n, src, dst, dev).start()

    def arrived(k, t, n, dst):
        copy(k, t, n // 3, n, dst, dst, sib).wait_recv()

    def sent(k, t, part, src):
        copy(k, t, part, 3 * part, src, src, sib).wait_send()

    def rows(slot, m, rhs):
        lhs = jnp.concatenate([xs[2 * m], xs[2 * m + 1]], axis=0)
        out = jnp.dot(lhs, rhs, preferred_element_type=F32).astype(BF16)
        for n in range(4):
            ps[slot, 0, m, n] = out[64 * n:64 * n + 64, :W]
            ps[slot, 1, n, m] = out[64 * n:64 * n + 64, W:]

    def stage0(k):
        rhs = weights(k)
        for m in range(4):
            rows(lax.rem(k, SL), m, rhs)
        send0(k)

    def push(k, t, n):
        slot = lax.rem(k, SL)
        f = first[t]
        r, l, o = up(f), down(f), opp(f)
        lo, hi = pl.ds(0, 2), pl.ds(2, 2)
        if n == 0:
            start(k, t, 0, ps.at[slot, t, o, lo], r1.at[slot, t, 0], dev_first(t, r))
        elif n == 1:
            start(k, t, 1, ps.at[slot, t, o, hi], r1.at[slot, t, 1], dev_first(t, l))
        elif n == 2:
            start(k, t, 2, ps.at[slot, t, r, hi], r2.at[slot, t, 0, hi], dev_first(t, r))
        else:
            start(k, t, 2, ps.at[slot, t, l, lo], r2.at[slot, t, 1, lo], dev_first(t, l))

    def send0(k):
        for t in range(2):
            for n in range(4):
                push(k, t, n)

    def stage1(k):
        slot = lax.rem(k, SL)
        for t in range(2):
            f = first[t]
            r, l = up(f), down(f)
            lo, hi = pl.ds(0, 2), pl.ds(2, 2)
            arrived(k, t, 0, r1.at[slot, t, 0])
            ps[slot, t, r, lo] = add2(ps[slot, t, r, lo], r1[slot, t, 0])
            start(k, t, 2, ps.at[slot, t, r, lo], r2.at[slot, t, 0, lo], dev_first(t, r))
            arrived(k, t, 1, r1.at[slot, t, 1])
            ps[slot, t, l, hi] = add2(ps[slot, t, l, hi], r1[slot, t, 1])
            start(k, t, 2, ps.at[slot, t, l, hi], r2.at[slot, t, 1, hi], dev_first(t, l))

    def stage2(k):
        slot = lax.rem(k, SL)
        for t in range(2):
            f, s = first[t], second[t]
            arrived(k, t, 2, r2.at[slot, t])
            qs[slot, t] = (
                ps[slot, t, f].astype(F32) + r2[slot, t, 0].astype(F32) + r2[slot, t, 1].astype(F32)
            ).astype(BF16)
            sent(k, t, 0, ps.at[slot, t, pl.ds(0, 3)])
            r, l, o = up(s), down(s), opp(s)
            lo, hi = pl.ds(0, 32), pl.ds(32, 32)
            start(k, t, 3, qs.at[slot, t, o, lo], t1.at[slot, t, 0], dev_second(t, r))
            start(k, t, 4, qs.at[slot, t, o, hi], t1.at[slot, t, 1], dev_second(t, l))
            start(k, t, 5, qs.at[slot, t, r, hi], t2.at[slot, t, 0, hi], dev_second(t, r))
            start(k, t, 5, qs.at[slot, t, l, lo], t2.at[slot, t, 1, lo], dev_second(t, l))

    def stage3(k):
        slot = lax.rem(k, SL)
        for t in range(2):
            s = second[t]
            r, l = up(s), down(s)
            lo, hi = pl.ds(0, 32), pl.ds(32, 32)
            arrived(k, t, 3, t1.at[slot, t, 0])
            qs[slot, t, r, lo] = add2(qs[slot, t, r, lo], t1[slot, t, 0])
            start(k, t, 5, qs.at[slot, t, r, lo], t2.at[slot, t, 0, lo], dev_second(t, r))
            arrived(k, t, 4, t1.at[slot, t, 1])
            qs[slot, t, l, hi] = add2(qs[slot, t, l, hi], t1[slot, t, 1])
            start(k, t, 5, qs.at[slot, t, l, hi], t2.at[slot, t, 1, hi], dev_second(t, l))

    def stage4(k):
        slot = lax.rem(k, SL)
        for t in range(2):
            f, s = first[t], second[t]
            arrived(k, t, 5, t2.at[slot, t])
            pre = qs[slot, t, s].astype(F32) + t2[slot, t, 0].astype(F32) + t2[slot, t, 1].astype(F32)
            cdf = 0.5 * (1.0 + lax.erf(pre * INV_ROOT_TWO))
            cols = pl.ds(pl.multiple_of((2 * k + t) * W, W), W)
            slope = cdf + pre * jnp.exp(-0.5 * pre * pre) * INV_ROOT_TAU
            gs[k, t, f, s] = (gact[:, cols].astype(F32) * slope).astype(BF16)
            sent(k, t, 1, qs.at[slot, t, pl.ds(0, 3)])
            start(k, t, 6, gs.at[k, t, f, s], gs.at[k, t, f, s], dev_second(t, up(s)))
            start(k, t, 7, gs.at[k, t, f, s], gs.at[k, t, f, s], dev_second(t, down(s)))

            @pl.when(k >= SL)
            def _():
                pltpu.make_async_copy(act.at[slot, t], act_hbm.at[:, cols], osem.at[slot, t]).wait()

            act[slot, t] = (pre * cdf).astype(BF16)
            pltpu.make_async_copy(act.at[slot, t], act_hbm.at[:, cols], osem.at[slot, t]).start()

    def stage5(k):
        for t in range(2):
            f, s = first[t], second[t]
            r, l = up(s), down(s)
            lo, hi = pl.ds(0, 32), pl.ds(32, 32)
            arrived(k, t, 6, gs.at[k, t, f, l])
            start(k, t, 8, gs.at[k, t, f, l, lo], gs.at[k, t, f, l, lo], dev_second(t, r))
            arrived(k, t, 7, gs.at[k, t, f, r])
            start(k, t, 8, gs.at[k, t, f, r, hi], gs.at[k, t, f, r, hi], dev_second(t, l))

    def stage6(k):
        for t in range(2):
            f, s = first[t], second[t]
            arrived(k, t, 8, gs.at[k, t, f, opp(s)])
            start(k, t, 9, gs.at[k, t, f], gs.at[k, t, f], dev_first(t, up(f)))
            start(k, t, 10, gs.at[k, t, f], gs.at[k, t, f], dev_first(t, down(f)))

    def stage7(k):
        for t in range(2):
            f = first[t]
            r, l = up(f), down(f)
            lo, hi = pl.ds(0, 2), pl.ds(2, 2)
            arrived(k, t, 9, gs.at[k, t, l])
            start(k, t, 11, gs.at[k, t, l, lo], gs.at[k, t, l, lo], dev_first(t, r))
            arrived(k, t, 10, gs.at[k, t, r])
            start(k, t, 11, gs.at[k, t, r, hi], gs.at[k, t, r, hi], dev_first(t, l))

    def gw_copies(k):
        g = lax.rem(k, 2)
        return [
            pltpu.make_async_copy(
                gwst.at[g, r], gw_hbm.at[pl.ds(r * CBK + 2 * WB * k, 2 * WB)], gsem.at[g, r]
            )
            for r in range(RB)
        ]

    def arrive8(k):
        for t in range(2):
            f = first[t]
            arrived(k, t, 11, gs.at[k, t, opp(f)])
            sent(k, t, 2, gs.at[k, t, f, pl.ds(0, 3)])
            sent(k, t, 3, gs.at[k, t, pl.ds(0, 3)])

    def whole_g(k):
        g0 = jnp.concatenate([gs[k, 0, n // 4, n % 4] for n in range(16)], axis=0)
        g1 = jnp.concatenate([gs[k, 1, n % 4, n // 4] for n in range(16)], axis=0)
        return jnp.concatenate([g0, g1], axis=1)

    def slot_grads(k, g):
        @pl.when(k >= 2)
        def _():
            for d in gw_copies(k - 2):
                d.wait()

        wg = jnp.dot(xt[...], g, preferred_element_type=F32).astype(BF16)
        for r in range(RB):
            for j in range(2 * WB):
                gwst[lax.rem(k, 2), r, j] = wg[r * BLK:(r + 1) * BLK, j * BLK:(j + 1) * BLK]
        for d in gw_copies(k):
            d.start()

    def stage8(k):
        arrive8(k)
        g = whole_g(k)
        term = lax.dot_general(
            g, weights(k), (((1,), (1,)), ((), ())), preferred_element_type=F32
        )
        dxa[...] += term.reshape(8, BLK, RB * BLK)
        slot_grads(k, g)

    stages = (stage0, stage1, stage2, stage3, stage4, stage5, stage6, stage7, stage8)

    def early(j):
        for k in range(EARLY):
            rows(k, j, weights(k))
            o = opp(xr)

            @pl.when(o == j)
            def _():
                push(k, 0, 0)
                push(k, 0, 1)

            @pl.when(up(xr) == j)
            def _():
                push(k, 0, 2)

            @pl.when(down(xr) == j)
            def _():
                push(k, 0, 3)

            if j == 0:
                push(k, 1, 0)
                push(k, 1, 3)
            if j == 3:
                push(k, 1, 1)
                push(k, 1, 2)

    for n in range(2):
        got(n, xq(0, c, n))
        go(0, 9 + n, xq(0, c, n), xq(3, c, n), zr_dev)
        got(6 + n, xq(2, c, n + 2))
        go(0, 11 + n, xq(2, c, n + 2), xq(3, c, n + 2), zl_dev)
        go(0, 13, xq(0, c, n), xq(0, c, n), sib)
        go(0, 14, xq(2, c, n + 2), xq(2, c, n + 2), sib)
    for n in range(2):
        got(2 + n, xq(0, c, n + 2))
        go(0, 13, xq(0, c, n + 2), xq(0, c, n + 2), sib)
        got(4 + n, xq(2, c, n))
        go(0, 14, xq(2, c, n), xq(2, c, n), sib)
    early(1)
    for n in range(2):
        got(9 + n, xq(3, c, n))
        go(0, 15, xq(3, c, n), xq(3, c, n), sib)
        got(11 + n, xq(3, c, n + 2))
        go(0, 15, xq(3, c, n + 2), xq(3, c, n + 2), sib)
    got(13, xs.at[1 - c])
    early(0)
    got(14, xs.at[4 + 1 - c])
    early(2)
    got(15, xs.at[6 + 1 - c])
    early(3)
    ac(0, 0, xs.at[pl.ds(0, 7)], xs.at[pl.ds(0, 7)], sib).wait_send()
    gcopy.wait()

    def body(i, carry):
        @pl.when(i == 2)
        def _():
            for r in range(RB):
                for q in range(8):
                    xt[r * BLK:(r + 1) * BLK, q * BLK:(q + 1) * BLK] = xs[q, :, r * BLK:(r + 1) * BLK].T

        for n in range(len(stages) - 1, -1, -1):
            k = i - n

            @pl.when((k >= (0 if n else EARLY)) & (k < NCH))
            def _():
                stages[n](k)

        return carry

    lax.fori_loop(1, NCH + len(stages) - 2, body, 0)

    last = NCH - 1
    arrive8(last)
    rhs = weights(last)
    for q in (3, 2, 0, 1):
        g0 = jnp.concatenate([gs[last, 0, q, m] for m in range(4)], axis=0)
        g1 = jnp.concatenate([gs[last, 1, m, q] for m in range(4)], axis=0)
        g = jnp.concatenate([g0, g1], axis=1)
        term = lax.dot_general(g, rhs, (((1,), (1,)), ((), ())), preferred_element_type=F32)
        dxa[2 * q:2 * q + 2] += term.reshape(2, BLK, RB * BLK)
        sb[q] = dxa[2 * q + (1 - c)].astype(BF16)
        go(1, 16 + q, sb.at[q], sr.at[q], sib)
    lo, hi = pl.ds(0, 64), pl.ds(64, 64)

    def join(q):
        got(16 + q, sr.at[q])
        eb[q] = (dxa[2 * q + c] + sr[q].astype(F32)).astype(BF16)

    join(3)
    go(1, 20, eb.at[3, lo], u1.at[0], zr_dev)
    go(1, 21, eb.at[3, hi], u1.at[1], zl_dev)
    join(2)
    go(1, 22, eb.at[2, hi], u2.at[0, hi], zr_dev)
    join(0)
    go(1, 22, eb.at[0, lo], u2.at[1, lo], zl_dev)
    join(1)
    got(20, u1.at[0])
    eb[2, lo] = add2(eb[2, lo], u1[0])
    go(1, 22, eb.at[2, lo], u2.at[0, lo], zr_dev)
    got(21, u1.at[1])
    eb[0, hi] = add2(eb[0, hi], u1[1])
    go(1, 22, eb.at[0, hi], u2.at[1, hi], zl_dev)
    slot_grads(last, whole_g(last))
    for k in range(NCH - SL, NCH):
        for t in range(2):
            cols = pl.ds((2 * k + t) * W, W)
            pltpu.make_async_copy(
                act.at[k % SL, t], act_hbm.at[:, cols], osem.at[k % SL, t]
            ).wait()
    for k in (last - 1, last):
        for d in gw_copies(k):
            d.wait()
    got(22, u2)
    dx_out[...] = eb[1].astype(F32) + u2[0].astype(F32) + u2[1].astype(F32)
    ac(1, 0, xs.at[pl.ds(0, 7)], xs.at[pl.ds(0, 7)], sib).wait_send()


def pick_kernel(rows, cols, count, act_in, dx_in, gwd, act, dx, gw, abuf, dbuf, gbuf, obuf, sem, gsem, osem):
    row0 = lax.axis_index("inb") * RB
    col0 = lax.axis_index("outb") * CBK

    def fetch(s):
        cell = (rows[s] - row0) * CBK + cols[s] - col0
        return pltpu.make_async_copy(gwd.at[cell], gbuf.at[s], gsem.at[s // 8])

    def begin(s, carry):
        fetch(s).start()
        return carry

    lax.fori_loop(0, CAP, begin, 0, unroll=4)
    ins = [
        pltpu.make_async_copy(act_in, abuf, sem.at[0]),
        pltpu.make_async_copy(dx_in, dbuf, sem.at[1]),
    ]
    for d in ins:
        d.start()
    outs = [
        pltpu.make_async_copy(abuf, act, sem.at[2]),
        pltpu.make_async_copy(dbuf, dx, sem.at[3]),
    ]

    def flush(n):
        return pltpu.make_async_copy(
            obuf.at[pl.ds(n * 8, 8)], gw.at[pl.ds(n * 8, 8)], osem.at[n]
        )

    def group(n, carry):
        group8 = pl.ds(n * 8, 8)
        pltpu.make_async_copy(gwd.at[group8], gbuf.at[group8], gsem.at[n]).wait()
        for m in range(8):
            s = n * 8 + m
            alive = (s < count[0, 0]).astype(F32)
            obuf[s] = gbuf[s].astype(F32) * alive
        flush(n).start()
        return carry

    lax.fori_loop(0, CAP // 8, group, 0)
    for d, e in zip(ins, outs):
        d.wait()
        e.start()

    def done(n, carry):
        flush(n).wait()
        return carry

    lax.fori_loop(0, CAP // 8, done, 0)
    for e in outs:
        e.wait()


def per_device(tokens, weight_blocks, block_rows, block_cols, block_count, grad_act):
    vmem = pl.BlockSpec(memory_space=pltpu.VMEM)
    smem = pl.BlockSpec(memory_space=pltpu.SMEM)
    hbm = pl.BlockSpec(memory_space=pl.ANY)
    rows, cols, count = block_rows[0, 0], block_cols[0, 0], block_count
    act_shape = jax.ShapeDtypeStruct((64, CBK * BLK), BF16)
    dx_shape = jax.ShapeDtypeStruct((BLK, RB * BLK), F32)
    act, dx, gwd = pl.pallas_call(
        kernel,
        out_shape=(
            act_shape,
            dx_shape,
            jax.ShapeDtypeStruct((RB * CBK, BLK, BLK), BF16),
        ),
        in_specs=[smem, smem, smem, hbm, hbm, hbm],
        out_specs=(hbm, vmem, hbm),
        scratch_shapes=[
            pltpu.SMEM((8, BLK), jnp.int32),
            pltpu.VMEM((8, BLK), jnp.int32),
            pltpu.VMEM((CAP + 1, BLK, BLK), BF16),
            pltpu.VMEM((8, BLK, RB * BLK), BF16),
            pltpu.VMEM((RB * BLK, 1024), BF16),
            pltpu.VMEM((SL, 2, 4, 4, 64, W), BF16),
            pltpu.VMEM((SL, 2, 2, 2, 64, W), BF16),
            pltpu.VMEM((SL, 2, 2, 4, 64, W), BF16),
            pltpu.VMEM((SL, 2, 4, 64, W), BF16),
            pltpu.VMEM((SL, 2, 2, 32, W), BF16),
            pltpu.VMEM((SL, 2, 2, 64, W), BF16),
            pltpu.VMEM((NCH, 2, 4, 4, 64, W), BF16),
            pltpu.VMEM((8, BLK, RB * BLK), F32),
            pltpu.VMEM((64, CBK * BLK), BF16),
            pltpu.VMEM((SL, 2, 64, W), BF16),
            pltpu.VMEM((2, RB, 2 * WB, BLK, BLK), BF16),
            pltpu.VMEM((4, BLK, RB * BLK), BF16),
            pltpu.VMEM((4, BLK, RB * BLK), BF16),
            pltpu.VMEM((4, BLK, RB * BLK), BF16),
            pltpu.VMEM((2, 64, RB * BLK), BF16),
            pltpu.VMEM((2, BLK, RB * BLK), BF16),
            pltpu.SemaphoreType.DMA((SL, 2, 4)),
            pltpu.SemaphoreType.DMA((SL, 2, 12)),
            pltpu.SemaphoreType.DMA((2,)),
            pltpu.SemaphoreType.DMA((23,)),
            pltpu.SemaphoreType.DMA((4,)),
            pltpu.SemaphoreType.DMA((SL, 2)),
            pltpu.SemaphoreType.DMA((2, RB)),
        ],
        compiler_params=pltpu.CompilerParams(
            collective_id=0, has_side_effects=True, vmem_limit_bytes=67043328
        ),
        name="ffn",
    )(rows, cols, count, tokens, weight_blocks[0, 0], grad_act)
    act, dx, gw = pl.pallas_call(
        pick_kernel,
        out_shape=(act_shape, dx_shape, jax.ShapeDtypeStruct((CAP, BLK, BLK), F32)),
        in_specs=[smem, smem, smem, hbm, hbm, hbm],
        out_specs=(hbm, hbm, hbm),
        scratch_shapes=[
            pltpu.VMEM(act_shape.shape, BF16),
            pltpu.VMEM(dx_shape.shape, F32),
            pltpu.VMEM((CAP, BLK, BLK), BF16),
            pltpu.VMEM((CAP, BLK, BLK), F32),
            pltpu.SemaphoreType.DMA((4,)),
            pltpu.SemaphoreType.DMA((CAP // 8,)),
            pltpu.SemaphoreType.DMA((CAP // 8,)),
        ],
        compiler_params=pltpu.CompilerParams(vmem_limit_bytes=67043328),
        name="pick",
    )(rows, cols, count, act, dx, gwd)
    return (act, dx, gw[None, None])


def solution(mesh):
    in_specs = (
        P("outb", "inb"),
        P("inb", "outb", None, None, None),
        P("inb", "outb", None),
        P("inb", "outb", None),
        P("inb", "outb"),
        P("inb", "outb"),
    )
    out_specs = (P("inb", "outb"), P("outb", "inb"), P("inb", "outb", None, None, None))
    return jax.shard_map(
        per_device, mesh=mesh, in_specs=in_specs, out_specs=out_specs, check_vma=False
    )
```

```python
import functools

import jax
import jax.numpy as jnp
from jax import lax
from jax.experimental import pallas as pl
from jax.experimental.pallas import tpu as pltpu
from jax.sharding import PartitionSpec as P

MESH = pl.DeviceIdType.MESH
F32 = jnp.float32
BF16 = jnp.bfloat16
INV_ROOT_TWO = 0.7071067811865476
INV_ROOT_TAU = 0.3989422804014327
BLK = 128
RB = 6
CBK = 48
CAP = 72
WB = 3
W = WB * BLK
NCH = CBK // (2 * WB)
SL = 4
EARLY = 1


def add2(a, b):
    return (a.astype(F32) + b.astype(F32)).astype(BF16)


def kernel(
    rows_in, cols_in, count_in, tok, wblk, gact_hbm,
    act_hbm, dx_out, gw_hbm,
    idx, tbl,
    wp, xs, xt, ps, r1, r2, qs, t1, t2, gs, dxa, gact, act, gwst, sb, sr, eb, u1, u2,
    ssem, rsem, asem, arsem, lsem, osem, gsem,
):
    a = lax.axis_index("inb")
    b = lax.axis_index("outb")
    x, y = a // 4, a % 4
    z, c = b // 2, b % 2

    def up(v):
        return lax.rem(v + 1, 4)

    def down(v):
        return lax.rem(v + 3, 4)

    def opp(v):
        return lax.rem(v + 2, 4)

    zr, zl = up(z), down(z)
    sib = (a, 2 * z + (1 - c))
    zr_dev, zl_dev = (a, 2 * zr + c), (a, 2 * zl + c)

    xr = lax.rem(x - z + 5, 4)
    first = (xr, y)
    second = (y, xr)

    def dev_x(v):
        return (4 * lax.rem(v + z + 3, 4) + y, b)

    def dev_y(v):
        return (4 * x + v, b)

    def dev_first(t, v):
        return dev_x(v) if t == 0 else dev_y(v)

    def dev_second(t, v):
        return dev_y(v) if t == 0 else dev_x(v)

    wcopy = pltpu.make_async_copy(wblk, wp.at[pl.ds(0, CAP)], lsem.at[0])
    wcopy.start()
    xcopy = pltpu.make_async_copy(tok, xs.at[2 + c], lsem.at[1])
    xcopy.start()
    gcopy = pltpu.make_async_copy(gact_hbm, gact, lsem.at[2])
    gcopy.start()

    barrier = pltpu.get_barrier_semaphore()
    for dev in (
        dev_x(up(xr)), dev_x(down(xr)), dev_y(up(y)), dev_y(down(y)),
        zr_dev, zl_dev, sib,
    ):
        pl.semaphore_signal(barrier, inc=1, device_id=dev, device_id_type=MESH)
    wp[CAP] = jnp.zeros((BLK, BLK), BF16)

    flat = BLK * lax.broadcasted_iota(jnp.int32, (8, BLK), 0) + lax.broadcasted_iota(jnp.int32, (8, BLK), 1)

    def place(n, found):
        cell = (rows_in[n] - a * RB) * CBK + cols_in[n] - b * CBK
        cell = jnp.where(n < count_in[0, 0], cell, 8 * BLK)
        return jnp.where(flat == cell, n, found)

    tbl[...] = lax.fori_loop(0, CAP, place, jnp.full((8, BLK), CAP, jnp.int32), unroll=4)
    tcopy = pltpu.make_async_copy(tbl, idx, lsem.at[3])
    tcopy.start()
    pl.semaphore_wait(barrier, 7)

    def ac(part, n, src, dst, dev):
        return pltpu.make_async_remote_copy(
            src_ref=src, dst_ref=dst, send_sem=asem.at[part], recv_sem=arsem.at[n],
            device_id=dev, device_id_type=MESH,
        )

    def go(part, n, src, dst, dev):
        ac(part, n, src, dst, dev).start()

    def got(n, dst):
        ac(0, n, dst, dst, sib).wait_recv()

    def xq(j, cc, h):
        return xs.at[2 * j + cc, pl.ds(32 * h, 32)]

    xcopy.wait()
    for n in range(4):
        m = (n + 2) % 4
        go(0, n, xq(1, c, n), xq(0, c, n), zr_dev)
        go(0, 4 + m, xq(1, c, m), xq(2, c, m), zl_dev)
    go(0, 8, xs.at[2 + c], xs.at[2 + c], sib)
    dxa[...] = jnp.zeros_like(dxa)
    wcopy.wait()
    tcopy.wait()
    got(8, xs.at[2 + 1 - c])

    def weights(k):
        cols = []
        for j in range(2 * WB):
            col = 2 * WB * k + j
            cols.append(jnp.concatenate([wp[idx[(r * CBK + col) // BLK, (r * CBK + col) % BLK]] for r in range(RB)], axis=0))
        return jnp.concatenate(cols, axis=1)

    def copy(k, t, part, n, src, dst, dev):
        slot = lax.rem(k, SL)
        return pltpu.make_async_remote_copy(
            src_ref=src, dst_ref=dst,
            send_sem=ssem.at[slot, t, part], recv_sem=rsem.at[slot, t, n],
            device_id=dev, device_id_type=MESH,
        )

    def start(k, t, n, src, dst, dev):
        copy(k, t, n // 3, n, src, dst, dev).start()

    def arrived(k, t, n, dst):
        copy(k, t, n // 3, n, dst, dst, sib).wait_recv()

    def sent(k, t, part, src):
        copy(k, t, part, 3 * part, src, src, sib).wait_send()

    def rows(slot, m, rhs):
        lhs = jnp.concatenate([xs[2 * m], xs[2 * m + 1]], axis=0)
        out = jnp.dot(lhs, rhs, preferred_element_type=F32).astype(BF16)
        for n in range(4):
            ps[slot, 0, m, n] = out[64 * n:64 * n + 64, :W]
            ps[slot, 1, n, m] = out[64 * n:64 * n + 64, W:]

    def stage0(k):
        rhs = weights(k)
        for m in range(4):
            rows(lax.rem(k, SL), m, rhs)
        send0(k)

    def push(k, t, n):
        slot = lax.rem(k, SL)
        f = first[t]
        r, l, o = up(f), down(f), opp(f)
        lo, hi = pl.ds(0, 2), pl.ds(2, 2)
        if n == 0:
            start(k, t, 0, ps.at[slot, t, o, lo], r1.at[slot, t, 0], dev_first(t, r))
        elif n == 1:
            start(k, t, 1, ps.at[slot, t, o, hi], r1.at[slot, t, 1], dev_first(t, l))
        elif n == 2:
            start(k, t, 2, ps.at[slot, t, r, hi], r2.at[slot, t, 0, hi], dev_first(t, r))
        else:
            start(k, t, 2, ps.at[slot, t, l, lo], r2.at[slot, t, 1, lo], dev_first(t, l))

    def send0(k):
        for t in range(2):
            for n in range(4):
                push(k, t, n)

    def stage1(k):
        slot = lax.rem(k, SL)
        for t in range(2):
            f = first[t]
            r, l = up(f), down(f)
            lo, hi = pl.ds(0, 2), pl.ds(2, 2)
            arrived(k, t, 0, r1.at[slot, t, 0])
            ps[slot, t, r, lo] = add2(ps[slot, t, r, lo], r1[slot, t, 0])
            start(k, t, 2, ps.at[slot, t, r, lo], r2.at[slot, t, 0, lo], dev_first(t, r))
            arrived(k, t, 1, r1.at[slot, t, 1])
            ps[slot, t, l, hi] = add2(ps[slot, t, l, hi], r1[slot, t, 1])
            start(k, t, 2, ps.at[slot, t, l, hi], r2.at[slot, t, 1, hi], dev_first(t, l))

    def stage2(k):
        slot = lax.rem(k, SL)
        for t in range(2):
            f, s = first[t], second[t]
            arrived(k, t, 2, r2.at[slot, t])
            qs[slot, t] = (
                ps[slot, t, f].astype(F32) + r2[slot, t, 0].astype(F32) + r2[slot, t, 1].astype(F32)
            ).astype(BF16)
            sent(k, t, 0, ps.at[slot, t, pl.ds(0, 3)])
            r, l, o = up(s), down(s), opp(s)
            lo, hi = pl.ds(0, 32), pl.ds(32, 32)
            start(k, t, 3, qs.at[slot, t, o, lo], t1.at[slot, t, 0], dev_second(t, r))
            start(k, t, 4, qs.at[slot, t, o, hi], t1.at[slot, t, 1], dev_second(t, l))

    def stage3(k):
        slot = lax.rem(k, SL)
        for t in range(2):
            s = second[t]
            r, l = up(s), down(s)
            lo, hi = pl.ds(0, 32), pl.ds(32, 32)
            arrived(k, t, 3, t1.at[slot, t, 0])
            qs[slot, t, r, lo] = add2(qs[slot, t, r, lo], t1[slot, t, 0])
            start(k, t, 5, qs.at[slot, t, r], t2.at[slot, t, 0], dev_second(t, r))
            arrived(k, t, 4, t1.at[slot, t, 1])
            qs[slot, t, l, hi] = add2(qs[slot, t, l, hi], t1[slot, t, 1])
            start(k, t, 5, qs.at[slot, t, l], t2.at[slot, t, 1], dev_second(t, l))

    def stage4(k):
        slot = lax.rem(k, SL)
        for t in range(2):
            f, s = first[t], second[t]
            arrived(k, t, 5, t2.at[slot, t])
            pre = qs[slot, t, s].astype(F32) + t2[slot, t, 0].astype(F32) + t2[slot, t, 1].astype(F32)
            cdf = 0.5 * (1.0 + lax.erf(pre * INV_ROOT_TWO))
            cols = pl.ds(pl.multiple_of((2 * k + t) * W, W), W)
            slope = cdf + pre * jnp.exp(-0.5 * pre * pre) * INV_ROOT_TAU
            gs[k, t, f, s] = (gact[:, cols].astype(F32) * slope).astype(BF16)
            sent(k, t, 1, qs.at[slot, t, pl.ds(0, 3)])
            start(k, t, 6, gs.at[k, t, f, s], gs.at[k, t, f, s], dev_second(t, up(s)))
            start(k, t, 7, gs.at[k, t, f, s], gs.at[k, t, f, s], dev_second(t, down(s)))

            @pl.when(k >= SL)
            def _():
                pltpu.make_async_copy(act.at[slot, t], act_hbm.at[:, cols], osem.at[slot, t]).wait()

            act[slot, t] = (pre * cdf).astype(BF16)
            pltpu.make_async_copy(act.at[slot, t], act_hbm.at[:, cols], osem.at[slot, t]).start()

    def stage5(k):
        for t in range(2):
            f, s = first[t], second[t]
            r, l = up(s), down(s)
            lo, hi = pl.ds(0, 32), pl.ds(32, 32)
            arrived(k, t, 6, gs.at[k, t, f, l])
            start(k, t, 8, gs.at[k, t, f, l, lo], gs.at[k, t, f, l, lo], dev_second(t, r))
            arrived(k, t, 7, gs.at[k, t, f, r])
            start(k, t, 8, gs.at[k, t, f, r, hi], gs.at[k, t, f, r, hi], dev_second(t, l))

    def stage6(k):
        for t in range(2):
            f, s = first[t], second[t]
            arrived(k, t, 8, gs.at[k, t, f, opp(s)])
            start(k, t, 9, gs.at[k, t, f], gs.at[k, t, f], dev_first(t, up(f)))
            start(k, t, 10, gs.at[k, t, f], gs.at[k, t, f], dev_first(t, down(f)))

    def stage7(k):
        for t in range(2):
            f = first[t]
            r, l = up(f), down(f)
            lo, hi = pl.ds(0, 2), pl.ds(2, 2)
            sent(k, t, 2, gs.at[k, t, f, pl.ds(0, 3)])
            arrived(k, t, 9, gs.at[k, t, l])
            start(k, t, 11, gs.at[k, t, l, lo], gs.at[k, t, l, lo], dev_first(t, r))
            arrived(k, t, 10, gs.at[k, t, r])
            start(k, t, 11, gs.at[k, t, r, hi], gs.at[k, t, r, hi], dev_first(t, l))

    def gw_copies(k):
        g = lax.rem(k, 2)
        return [
            pltpu.make_async_copy(
                gwst.at[g, r], gw_hbm.at[pl.ds(r * CBK + 2 * WB * k, 2 * WB)], gsem.at[g, r]
            )
            for r in range(RB)
        ]

    def arrive8(k):
        for t in range(2):
            f = first[t]
            arrived(k, t, 11, gs.at[k, t, opp(f)])
            sent(k, t, 3, gs.at[k, t, pl.ds(0, 3)])

    def whole_g(k):
        g0 = jnp.concatenate([gs[k, 0, n // 4, n % 4] for n in range(16)], axis=0)
        g1 = jnp.concatenate([gs[k, 1, n % 4, n // 4] for n in range(16)], axis=0)
        return jnp.concatenate([g0, g1], axis=1)

    def slot_grads(k, g):
        @pl.when(k >= 2)
        def _():
            for d in gw_copies(k - 2):
                d.wait()

        wg = jnp.dot(xt[...], g, preferred_element_type=F32).astype(BF16)
        for r in range(RB):
            for j in range(2 * WB):
                gwst[lax.rem(k, 2), r, j] = wg[r * BLK:(r + 1) * BLK, j * BLK:(j + 1) * BLK]
        for d in gw_copies(k):
            d.start()

    def stage8(k):
        arrive8(k)
        g = whole_g(k)
        term = lax.dot_general(
            g, weights(k), (((1,), (1,)), ((), ())), preferred_element_type=F32
        )
        dxa[...] += term.reshape(8, BLK, RB * BLK)
        slot_grads(k, g)

    stages = (stage0, stage1, stage2, stage3, stage4, stage5, stage6, stage7, stage8)

    def early(j):
        for k in range(EARLY):
            rows(k, j, weights(k))
            o = opp(xr)

            @pl.when(o == j)
            def _():
                push(k, 0, 0)
                push(k, 0, 1)

            @pl.when(up(xr) == j)
            def _():
                push(k, 0, 2)

            @pl.when(down(xr) == j)
            def _():
                push(k, 0, 3)

            if j == 0:
                push(k, 1, 0)
                push(k, 1, 3)
            if j == 3:
                push(k, 1, 1)
                push(k, 1, 2)

    for n in range(2):
        got(n, xq(0, c, n))
        go(0, 9 + n, xq(0, c, n), xq(3, c, n), zr_dev)
        got(6 + n, xq(2, c, n + 2))
        go(0, 11 + n, xq(2, c, n + 2), xq(3, c, n + 2), zl_dev)
        go(0, 13, xq(0, c, n), xq(0, c, n), sib)
        go(0, 14, xq(2, c, n + 2), xq(2, c, n + 2), sib)
    for n in range(2):
        got(2 + n, xq(0, c, n + 2))
        go(0, 13, xq(0, c, n + 2), xq(0, c, n + 2), sib)
        got(4 + n, xq(2, c, n))
        go(0, 14, xq(2, c, n), xq(2, c, n), sib)
    early(1)
    for n in range(2):
        got(9 + n, xq(3, c, n))
        go(0, 15, xq(3, c, n), xq(3, c, n), sib)
        got(11 + n, xq(3, c, n + 2))
        go(0, 15, xq(3, c, n + 2), xq(3, c, n + 2), sib)
    got(13, xs.at[1 - c])
    early(0)
    got(14, xs.at[4 + 1 - c])
    early(2)
    got(15, xs.at[6 + 1 - c])
    early(3)
    ac(0, 0, xs.at[pl.ds(0, 7)], xs.at[pl.ds(0, 7)], sib).wait_send()
    gcopy.wait()

    def body(i, carry):
        @pl.when(i == 2)
        def _():
            for r in range(RB):
                for q in range(8):
                    xt[r * BLK:(r + 1) * BLK, q * BLK:(q + 1) * BLK] = xs[q, :, r * BLK:(r + 1) * BLK].T

        for n in (7, 6, 5, 4, 3, 2, 1, 0, 8):
            k = i - n

            @pl.when((k >= (0 if n else EARLY)) & (k < NCH))
            def _():
                stages[n](k)

        return carry

    lax.fori_loop(1, NCH + len(stages) - 2, body, 0)

    last = NCH - 1
    arrive8(last)
    rhs = weights(last)
    for q in (3, 2, 0, 1):
        g0 = jnp.concatenate([gs[last, 0, q, m] for m in range(4)], axis=0)
        g1 = jnp.concatenate([gs[last, 1, m, q] for m in range(4)], axis=0)
        g = jnp.concatenate([g0, g1], axis=1)
        term = lax.dot_general(g, rhs, (((1,), (1,)), ((), ())), preferred_element_type=F32)
        dxa[2 * q:2 * q + 2] += term.reshape(2, BLK, RB * BLK)
        sb[q] = dxa[2 * q + (1 - c)].astype(BF16)
        go(1, 16 + q, sb.at[q], sr.at[q], sib)
    lo, hi = pl.ds(0, 64), pl.ds(64, 64)

    def join(q):
        got(16 + q, sr.at[q])
        eb[q] = (dxa[2 * q + c] + sr[q].astype(F32)).astype(BF16)

    join(3)
    go(1, 20, eb.at[3, lo], u1.at[0], zr_dev)
    go(1, 21, eb.at[3, hi], u1.at[1], zl_dev)
    join(2)
    go(1, 22, eb.at[2, hi], u2.at[0, hi], zr_dev)
    join(0)
    go(1, 22, eb.at[0, lo], u2.at[1, lo], zl_dev)
    join(1)
    got(20, u1.at[0])
    eb[2, lo] = add2(eb[2, lo], u1[0])
    go(1, 22, eb.at[2, lo], u2.at[0, lo], zr_dev)
    got(21, u1.at[1])
    eb[0, hi] = add2(eb[0, hi], u1[1])
    go(1, 22, eb.at[0, hi], u2.at[1, hi], zl_dev)
    slot_grads(last, whole_g(last))
    for k in range(NCH - SL, NCH):
        for t in range(2):
            cols = pl.ds((2 * k + t) * W, W)
            pltpu.make_async_copy(
                act.at[k % SL, t], act_hbm.at[:, cols], osem.at[k % SL, t]
            ).wait()
    for k in (last - 1, last):
        for d in gw_copies(k):
            d.wait()
    got(22, u2)
    dx_out[...] = eb[1].astype(F32) + u2[0].astype(F32) + u2[1].astype(F32)
    ac(1, 0, xs.at[pl.ds(0, 7)], xs.at[pl.ds(0, 7)], sib).wait_send()


def pick_kernel(rows, cols, count, act_in, dx_in, gwd, act, dx, gw, abuf, dbuf, gbuf, obuf, sem, gsem, osem):
    row0 = lax.axis_index("inb") * RB
    col0 = lax.axis_index("outb") * CBK

    def fetch(s):
        cell = (rows[s] - row0) * CBK + cols[s] - col0
        return pltpu.make_async_copy(gwd.at[cell], gbuf.at[s], gsem.at[s // 8])

    def begin(s, carry):
        fetch(s).start()
        return carry

    lax.fori_loop(0, CAP, begin, 0, unroll=4)
    ins = [
        pltpu.make_async_copy(act_in, abuf, sem.at[0]),
        pltpu.make_async_copy(dx_in, dbuf, sem.at[1]),
    ]
    for d in ins:
        d.start()
    outs = [
        pltpu.make_async_copy(abuf, act, sem.at[2]),
        pltpu.make_async_copy(dbuf, dx, sem.at[3]),
    ]

    def flush(n):
        return pltpu.make_async_copy(
            obuf.at[pl.ds(n * 8, 8)], gw.at[pl.ds(n * 8, 8)], osem.at[n]
        )

    def group(n, carry):
        group8 = pl.ds(n * 8, 8)
        pltpu.make_async_copy(gwd.at[group8], gbuf.at[group8], gsem.at[n]).wait()
        for m in range(8):
            s = n * 8 + m
            alive = (s < count[0, 0]).astype(F32)
            obuf[s] = gbuf[s].astype(F32) * alive
        flush(n).start()
        return carry

    lax.fori_loop(0, CAP // 8, group, 0)
    for d, e in zip(ins, outs):
        d.wait()
        e.start()

    def done(n, carry):
        flush(n).wait()
        return carry

    lax.fori_loop(0, CAP // 8, done, 0)
    for e in outs:
        e.wait()


def per_device(tokens, weight_blocks, block_rows, block_cols, block_count, grad_act):
    vmem = pl.BlockSpec(memory_space=pltpu.VMEM)
    smem = pl.BlockSpec(memory_space=pltpu.SMEM)
    hbm = pl.BlockSpec(memory_space=pl.ANY)
    rows, cols, count = block_rows[0, 0], block_cols[0, 0], block_count
    act_shape = jax.ShapeDtypeStruct((64, CBK * BLK), BF16)
    dx_shape = jax.ShapeDtypeStruct((BLK, RB * BLK), F32)
    act, dx, gwd = pl.pallas_call(
        kernel,
        out_shape=(
            act_shape,
            dx_shape,
            jax.ShapeDtypeStruct((RB * CBK, BLK, BLK), BF16),
        ),
        in_specs=[smem, smem, smem, hbm, hbm, hbm],
        out_specs=(hbm, vmem, hbm),
        scratch_shapes=[
            pltpu.SMEM((8, BLK), jnp.int32),
            pltpu.VMEM((8, BLK), jnp.int32),
            pltpu.VMEM((CAP + 1, BLK, BLK), BF16),
            pltpu.VMEM((8, BLK, RB * BLK), BF16),
            pltpu.VMEM((RB * BLK, 1024), BF16),
            pltpu.VMEM((SL, 2, 4, 4, 64, W), BF16),
            pltpu.VMEM((SL, 2, 2, 2, 64, W), BF16),
            pltpu.VMEM((SL, 2, 2, 4, 64, W), BF16),
            pltpu.VMEM((SL, 2, 4, 64, W), BF16),
            pltpu.VMEM((SL, 2, 2, 32, W), BF16),
            pltpu.VMEM((SL, 2, 2, 64, W), BF16),
            pltpu.VMEM((NCH, 2, 4, 4, 64, W), BF16),
            pltpu.VMEM((8, BLK, RB * BLK), F32),
            pltpu.VMEM((64, CBK * BLK), BF16),
            pltpu.VMEM((SL, 2, 64, W), BF16),
            pltpu.VMEM((2, RB, 2 * WB, BLK, BLK), BF16),
            pltpu.VMEM((4, BLK, RB * BLK), BF16),
            pltpu.VMEM((4, BLK, RB * BLK), BF16),
            pltpu.VMEM((4, BLK, RB * BLK), BF16),
            pltpu.VMEM((2, 64, RB * BLK), BF16),
            pltpu.VMEM((2, BLK, RB * BLK), BF16),
            pltpu.SemaphoreType.DMA((SL, 2, 4)),
            pltpu.SemaphoreType.DMA((SL, 2, 12)),
            pltpu.SemaphoreType.DMA((2,)),
            pltpu.SemaphoreType.DMA((23,)),
            pltpu.SemaphoreType.DMA((4,)),
            pltpu.SemaphoreType.DMA((SL, 2)),
            pltpu.SemaphoreType.DMA((2, RB)),
        ],
        compiler_params=pltpu.CompilerParams(
            collective_id=0, has_side_effects=True, vmem_limit_bytes=67043328
        ),
        name="ffn",
    )(rows, cols, count, tokens, weight_blocks[0, 0], grad_act)
    act, dx, gw = pl.pallas_call(
        pick_kernel,
        out_shape=(act_shape, dx_shape, jax.ShapeDtypeStruct((CAP, BLK, BLK), F32)),
        in_specs=[smem, smem, smem, hbm, hbm, hbm],
        out_specs=(hbm, hbm, hbm),
        scratch_shapes=[
            pltpu.VMEM(act_shape.shape, BF16),
            pltpu.VMEM(dx_shape.shape, F32),
            pltpu.VMEM((CAP, BLK, BLK), BF16),
            pltpu.VMEM((CAP, BLK, BLK), F32),
            pltpu.SemaphoreType.DMA((4,)),
            pltpu.SemaphoreType.DMA((CAP // 8,)),
            pltpu.SemaphoreType.DMA((CAP // 8,)),
        ],
        compiler_params=pltpu.CompilerParams(vmem_limit_bytes=67043328),
        name="pick",
    )(rows, cols, count, act, dx, gwd)
    return (act, dx, gw[None, None])


def solution(mesh):
    in_specs = (
        P("outb", "inb"),
        P("inb", "outb", None, None, None),
        P("inb", "outb", None),
        P("inb", "outb", None),
        P("inb", "outb"),
        P("inb", "outb"),
    )
    out_specs = (P("inb", "outb"), P("outb", "inb"), P("inb", "outb", None, None, None))
    return jax.shard_map(
        per_device, mesh=mesh, in_specs=in_specs, out_specs=out_specs, check_vma=False
    )
```

```python
import functools

import jax
import jax.numpy as jnp
from jax import lax
from jax.experimental import pallas as pl
from jax.experimental.pallas import tpu as pltpu
from jax.sharding import PartitionSpec as P

MESH = pl.DeviceIdType.MESH
F32 = jnp.float32
BF16 = jnp.bfloat16
INV_ROOT_TWO = 0.7071067811865476
INV_ROOT_TAU = 0.3989422804014327
BLK = 128
RB = 6
CBK = 48
CAP = 72
WB = 3
W = WB * BLK
NCH = CBK // (2 * WB)
SL = 4
EARLY = 1


def add2(a, b):
    return (a.astype(F32) + b.astype(F32)).astype(BF16)


def kernel(
    rows_in, cols_in, count_in, tok, wblk, gact_hbm,
    act_hbm, dx_out, gw_hbm,
    idx, tbl,
    wp, xs, xt, ps, r1, r2, qs, t1, t2, gs, dxa, gact, act, gwst, sb, sr, eb, u1, u2,
    ssem, rsem, asem, arsem, lsem, osem, gsem,
):
    a = lax.axis_index("inb")
    b = lax.axis_index("outb")
    x, y = a // 4, a % 4
    z, c = b // 2, b % 2

    def up(v):
        return lax.rem(v + 1, 4)

    def down(v):
        return lax.rem(v + 3, 4)

    def opp(v):
        return lax.rem(v + 2, 4)

    zr, zl = up(z), down(z)
    sib = (a, 2 * z + (1 - c))
    zr_dev, zl_dev = (a, 2 * zr + c), (a, 2 * zl + c)

    xr = lax.rem(x - z + 5, 4)
    first = (xr, y)
    second = (y, xr)

    def dev_x(v):
        return (4 * lax.rem(v + z + 3, 4) + y, b)

    def dev_y(v):
        return (4 * x + v, b)

    def dev_first(t, v):
        return dev_x(v) if t == 0 else dev_y(v)

    def dev_second(t, v):
        return dev_y(v) if t == 0 else dev_x(v)

    wcopy = pltpu.make_async_copy(wblk, wp.at[pl.ds(0, CAP)], lsem.at[0])
    wcopy.start()
    xcopy = pltpu.make_async_copy(tok, xs.at[2 + c], lsem.at[1])
    xcopy.start()
    gcopy = pltpu.make_async_copy(gact_hbm, gact, lsem.at[2])
    gcopy.start()

    barrier = pltpu.get_barrier_semaphore()
    for dev in (
        dev_x(up(xr)), dev_x(down(xr)), dev_y(up(y)), dev_y(down(y)),
        zr_dev, zl_dev, sib,
    ):
        pl.semaphore_signal(barrier, inc=1, device_id=dev, device_id_type=MESH)
    wp[CAP] = jnp.zeros((BLK, BLK), BF16)

    flat = BLK * lax.broadcasted_iota(jnp.int32, (8, BLK), 0) + lax.broadcasted_iota(jnp.int32, (8, BLK), 1)

    def place(n, found):
        cell = (rows_in[n] - a * RB) * CBK + cols_in[n] - b * CBK
        cell = jnp.where(n < count_in[0, 0], cell, 8 * BLK)
        return jnp.where(flat == cell, n, found)

    tbl[...] = lax.fori_loop(0, CAP, place, jnp.full((8, BLK), CAP, jnp.int32), unroll=4)
    tcopy = pltpu.make_async_copy(tbl, idx, lsem.at[3])
    tcopy.start()
    pl.semaphore_wait(barrier, 7)

    def ac(part, n, src, dst, dev):
        return pltpu.make_async_remote_copy(
            src_ref=src, dst_ref=dst, send_sem=asem.at[part], recv_sem=arsem.at[n],
            device_id=dev, device_id_type=MESH,
        )

    def go(part, n, src, dst, dev):
        ac(part, n, src, dst, dev).start()

    def got(n, dst):
        ac(0, n, dst, dst, sib).wait_recv()

    def xq(j, cc, h):
        return xs.at[2 * j + cc, pl.ds(32 * h, 32)]

    xcopy.wait()
    for n in range(4):
        m = (n + 2) % 4
        go(0, n, xq(1, c, n), xq(0, c, n), zr_dev)
        go(0, 4 + m, xq(1, c, m), xq(2, c, m), zl_dev)
    go(0, 8, xs.at[2 + c], xs.at[2 + c], sib)
    dxa[...] = jnp.zeros_like(dxa)
    wcopy.wait()
    tcopy.wait()
    got(8, xs.at[2 + 1 - c])

    def weights(k):
        cols = []
        for j in range(2 * WB):
            col = 2 * WB * k + j
            cols.append(jnp.concatenate([wp[idx[(r * CBK + col) // BLK, (r * CBK + col) % BLK]] for r in range(RB)], axis=0))
        return jnp.concatenate(cols, axis=1)

    def copy(k, t, part, n, src, dst, dev):
        slot = lax.rem(k, SL)
        return pltpu.make_async_remote_copy(
            src_ref=src, dst_ref=dst,
            send_sem=ssem.at[slot, t, part], recv_sem=rsem.at[slot, t, n],
            device_id=dev, device_id_type=MESH,
        )

    def start(k, t, n, src, dst, dev):
        copy(k, t, n // 3, n, src, dst, dev).start()

    def arrived(k, t, n, dst):
        copy(k, t, n // 3, n, dst, dst, sib).wait_recv()

    def sent(k, t, part, src):
        copy(k, t, part, 3 * part, src, src, sib).wait_send()

    def rows(slot, m, rhs):
        lhs = jnp.concatenate([xs[2 * m], xs[2 * m + 1]], axis=0)
        out = jnp.dot(lhs, rhs, preferred_element_type=F32).astype(BF16)
        for n in range(4):
            ps[slot, 0, m, n] = out[64 * n:64 * n + 64, :W]
            ps[slot, 1, n, m] = out[64 * n:64 * n + 64, W:]

    def stage0(k):
        rhs = weights(k)
        for m in range(4):
            rows(lax.rem(k, SL), m, rhs)
        send0(k)

    def send0(k):
        slot = lax.rem(k, SL)
        for t in range(2):
            f = first[t]
            r, l, o = up(f), down(f), opp(f)
            lo, hi = pl.ds(0, 2), pl.ds(2, 2)
            start(k, t, 0, ps.at[slot, t, o, lo], r1.at[slot, t, 0], dev_first(t, r))
            start(k, t, 1, ps.at[slot, t, o, hi], r1.at[slot, t, 1], dev_first(t, l))
            start(k, t, 2, ps.at[slot, t, r, hi], r2.at[slot, t, 0, hi], dev_first(t, r))
            start(k, t, 2, ps.at[slot, t, l, lo], r2.at[slot, t, 1, lo], dev_first(t, l))

    def stage1(k):
        slot = lax.rem(k, SL)
        for t in range(2):
            f = first[t]
            r, l = up(f), down(f)
            lo, hi = pl.ds(0, 2), pl.ds(2, 2)
            arrived(k, t, 0, r1.at[slot, t, 0])
            ps[slot, t, r, lo] = add2(ps[slot, t, r, lo], r1[slot, t, 0])
            start(k, t, 2, ps.at[slot, t, r, lo], r2.at[slot, t, 0, lo], dev_first(t, r))
            arrived(k, t, 1, r1.at[slot, t, 1])
            ps[slot, t, l, hi] = add2(ps[slot, t, l, hi], r1[slot, t, 1])
            start(k, t, 2, ps.at[slot, t, l, hi], r2.at[slot, t, 1, hi], dev_first(t, l))

    def stage2(k):
        slot = lax.rem(k, SL)
        for t in range(2):
            f, s = first[t], second[t]
            arrived(k, t, 2, r2.at[slot, t])
            qs[slot, t] = (
                ps[slot, t, f].astype(F32) + r2[slot, t, 0].astype(F32) + r2[slot, t, 1].astype(F32)
            ).astype(BF16)
            sent(k, t, 0, ps.at[slot, t, pl.ds(0, 3)])
            r, l, o = up(s), down(s), opp(s)
            lo, hi = pl.ds(0, 32), pl.ds(32, 32)
            start(k, t, 3, qs.at[slot, t, o, lo], t1.at[slot, t, 0], dev_second(t, r))
            start(k, t, 4, qs.at[slot, t, o, hi], t1.at[slot, t, 1], dev_second(t, l))

    def stage3(k):
        slot = lax.rem(k, SL)
        for t in range(2):
            s = second[t]
            r, l = up(s), down(s)
            lo, hi = pl.ds(0, 32), pl.ds(32, 32)
            arrived(k, t, 3, t1.at[slot, t, 0])
            qs[slot, t, r, lo] = add2(qs[slot, t, r, lo], t1[slot, t, 0])
            start(k, t, 5, qs.at[slot, t, r], t2.at[slot, t, 0], dev_second(t, r))
            arrived(k, t, 4, t1.at[slot, t, 1])
            qs[slot, t, l, hi] = add2(qs[slot, t, l, hi], t1[slot, t, 1])
            start(k, t, 5, qs.at[slot, t, l], t2.at[slot, t, 1], dev_second(t, l))

    def stage4(k):
        slot = lax.rem(k, SL)
        for t in range(2):
            f, s = first[t], second[t]
            arrived(k, t, 5, t2.at[slot, t])
            pre = qs[slot, t, s].astype(F32) + t2[slot, t, 0].astype(F32) + t2[slot, t, 1].astype(F32)
            cdf = 0.5 * (1.0 + lax.erf(pre * INV_ROOT_TWO))
            cols = pl.ds(pl.multiple_of((2 * k + t) * W, W), W)
            slope = cdf + pre * jnp.exp(-0.5 * pre * pre) * INV_ROOT_TAU
            gs[k, t, f, s] = (gact[:, cols].astype(F32) * slope).astype(BF16)
            sent(k, t, 1, qs.at[slot, t, pl.ds(0, 3)])
            start(k, t, 6, gs.at[k, t, f, s], gs.at[k, t, f, s], dev_second(t, up(s)))
            start(k, t, 7, gs.at[k, t, f, s], gs.at[k, t, f, s], dev_second(t, down(s)))

            @pl.when(k >= SL)
            def _():
                pltpu.make_async_copy(act.at[slot, t], act_hbm.at[:, cols], osem.at[slot, t]).wait()

            act[slot, t] = (pre * cdf).astype(BF16)
            pltpu.make_async_copy(act.at[slot, t], act_hbm.at[:, cols], osem.at[slot, t]).start()

    def stage5(k):
        for t in range(2):
            f, s = first[t], second[t]
            r, l = up(s), down(s)
            lo, hi = pl.ds(0, 32), pl.ds(32, 32)
            arrived(k, t, 6, gs.at[k, t, f, l])
            start(k, t, 8, gs.at[k, t, f, l, lo], gs.at[k, t, f, l, lo], dev_second(t, r))
            arrived(k, t, 7, gs.at[k, t, f, r])
            start(k, t, 8, gs.at[k, t, f, r, hi], gs.at[k, t, f, r, hi], dev_second(t, l))

    def stage6(k):
        for t in range(2):
            f, s = first[t], second[t]
            arrived(k, t, 8, gs.at[k, t, f, opp(s)])
            start(k, t, 9, gs.at[k, t, f], gs.at[k, t, f], dev_first(t, up(f)))
            start(k, t, 10, gs.at[k, t, f], gs.at[k, t, f], dev_first(t, down(f)))

    def stage7(k):
        for t in range(2):
            f = first[t]
            r, l = up(f), down(f)
            lo, hi = pl.ds(0, 2), pl.ds(2, 2)
            sent(k, t, 2, gs.at[k, t, f, pl.ds(0, 3)])
            arrived(k, t, 9, gs.at[k, t, l])
            start(k, t, 11, gs.at[k, t, l, lo], gs.at[k, t, l, lo], dev_first(t, r))
            arrived(k, t, 10, gs.at[k, t, r])
            start(k, t, 11, gs.at[k, t, r, hi], gs.at[k, t, r, hi], dev_first(t, l))

    def gw_copies(k):
        g = lax.rem(k, 2)
        return [
            pltpu.make_async_copy(
                gwst.at[g, r], gw_hbm.at[pl.ds(r * CBK + 2 * WB * k, 2 * WB)], gsem.at[g, r]
            )
            for r in range(RB)
        ]

    def arrive8(k):
        for t in range(2):
            f = first[t]
            arrived(k, t, 11, gs.at[k, t, opp(f)])
            sent(k, t, 3, gs.at[k, t, pl.ds(0, 3)])

    def whole_g(k):
        g0 = jnp.concatenate([gs[k, 0, n // 4, n % 4] for n in range(16)], axis=0)
        g1 = jnp.concatenate([gs[k, 1, n % 4, n // 4] for n in range(16)], axis=0)
        return jnp.concatenate([g0, g1], axis=1)

    def slot_grads(k, g):
        @pl.when(k >= 2)
        def _():
            for d in gw_copies(k - 2):
                d.wait()

        wg = jnp.dot(xt[...], g, preferred_element_type=F32).astype(BF16)
        for r in range(RB):
            for j in range(2 * WB):
                gwst[lax.rem(k, 2), r, j] = wg[r * BLK:(r + 1) * BLK, j * BLK:(j + 1) * BLK]
        for d in gw_copies(k):
            d.start()

    def stage8(k):
        arrive8(k)
        g = whole_g(k)
        term = lax.dot_general(
            g, weights(k), (((1,), (1,)), ((), ())), preferred_element_type=F32
        )
        dxa[...] += term.reshape(8, BLK, RB * BLK)
        slot_grads(k, g)

    stages = (stage0, stage1, stage2, stage3, stage4, stage5, stage6, stage7, stage8)

    def early(j):
        for k in range(EARLY):
            rows(k, j, weights(k))

    for n in range(2):
        got(n, xq(0, c, n))
        go(0, 9 + n, xq(0, c, n), xq(3, c, n), zr_dev)
        got(6 + n, xq(2, c, n + 2))
        go(0, 11 + n, xq(2, c, n + 2), xq(3, c, n + 2), zl_dev)
        go(0, 13, xq(0, c, n), xq(0, c, n), sib)
        go(0, 14, xq(2, c, n + 2), xq(2, c, n + 2), sib)
    for n in range(2):
        got(2 + n, xq(0, c, n + 2))
        go(0, 13, xq(0, c, n + 2), xq(0, c, n + 2), sib)
        got(4 + n, xq(2, c, n))
        go(0, 14, xq(2, c, n), xq(2, c, n), sib)
    early(1)
    for n in range(2):
        got(9 + n, xq(3, c, n))
        go(0, 15, xq(3, c, n), xq(3, c, n), sib)
        got(11 + n, xq(3, c, n + 2))
        go(0, 15, xq(3, c, n + 2), xq(3, c, n + 2), sib)
    got(13, xs.at[1 - c])
    early(0)
    got(14, xs.at[4 + 1 - c])
    early(2)
    got(15, xs.at[6 + 1 - c])
    early(3)
    for k in range(EARLY):
        send0(k)
    ac(0, 0, xs.at[pl.ds(0, 7)], xs.at[pl.ds(0, 7)], sib).wait_send()
    gcopy.wait()

    def body(i, carry):
        @pl.when(i == 2)
        def _():
            for r in range(RB):
                for q in range(8):
                    xt[r * BLK:(r + 1) * BLK, q * BLK:(q + 1) * BLK] = xs[q, :, r * BLK:(r + 1) * BLK].T

        for n in (7, 6, 5, 4, 3, 2, 1, 0, 8):
            k = i - n

            @pl.when((k >= (0 if n else EARLY)) & (k < NCH))
            def _():
                stages[n](k)

        return carry

    lax.fori_loop(1, NCH + len(stages) - 2, body, 0)

    last = NCH - 1
    arrive8(last)
    rhs = weights(last)
    for q in (3, 2, 0, 1):
        g0 = jnp.concatenate([gs[last, 0, q, m] for m in range(4)], axis=0)
        g1 = jnp.concatenate([gs[last, 1, m, q] for m in range(4)], axis=0)
        g = jnp.concatenate([g0, g1], axis=1)
        term = lax.dot_general(g, rhs, (((1,), (1,)), ((), ())), preferred_element_type=F32)
        dxa[2 * q:2 * q + 2] += term.reshape(2, BLK, RB * BLK)
        sb[q] = dxa[2 * q + (1 - c)].astype(BF16)
        go(1, 16 + q, sb.at[q], sr.at[q], sib)
    lo, hi = pl.ds(0, 64), pl.ds(64, 64)

    def join(q):
        got(16 + q, sr.at[q])
        eb[q] = (dxa[2 * q + c] + sr[q].astype(F32)).astype(BF16)

    join(3)
    go(1, 20, eb.at[3, lo], u1.at[0], zr_dev)
    go(1, 21, eb.at[3, hi], u1.at[1], zl_dev)
    join(2)
    go(1, 22, eb.at[2, hi], u2.at[0, hi], zr_dev)
    join(0)
    go(1, 22, eb.at[0, lo], u2.at[1, lo], zl_dev)
    join(1)
    got(20, u1.at[0])
    eb[2, lo] = add2(eb[2, lo], u1[0])
    go(1, 22, eb.at[2, lo], u2.at[0, lo], zr_dev)
    got(21, u1.at[1])
    eb[0, hi] = add2(eb[0, hi], u1[1])
    go(1, 22, eb.at[0, hi], u2.at[1, hi], zl_dev)
    slot_grads(last, whole_g(last))
    for k in range(NCH - SL, NCH):
        for t in range(2):
            cols = pl.ds((2 * k + t) * W, W)
            pltpu.make_async_copy(
                act.at[k % SL, t], act_hbm.at[:, cols], osem.at[k % SL, t]
            ).wait()
    for k in (last - 1, last):
        for d in gw_copies(k):
            d.wait()
    got(22, u2)
    dx_out[...] = eb[1].astype(F32) + u2[0].astype(F32) + u2[1].astype(F32)
    ac(1, 0, xs.at[pl.ds(0, 7)], xs.at[pl.ds(0, 7)], sib).wait_send()


def pick_kernel(rows, cols, count, act_in, dx_in, gwd, act, dx, gw, abuf, dbuf, gbuf, obuf, sem, gsem, osem):
    row0 = lax.axis_index("inb") * RB
    col0 = lax.axis_index("outb") * CBK

    def fetch(s):
        cell = (rows[s] - row0) * CBK + cols[s] - col0
        return pltpu.make_async_copy(gwd.at[cell], gbuf.at[s], gsem.at[s // 8])

    def begin(s, carry):
        fetch(s).start()
        return carry

    lax.fori_loop(0, CAP, begin, 0, unroll=4)
    ins = [
        pltpu.make_async_copy(act_in, abuf, sem.at[0]),
        pltpu.make_async_copy(dx_in, dbuf, sem.at[1]),
    ]
    for d in ins:
        d.start()
    outs = [
        pltpu.make_async_copy(abuf, act, sem.at[2]),
        pltpu.make_async_copy(dbuf, dx, sem.at[3]),
    ]

    def flush(n):
        return pltpu.make_async_copy(
            obuf.at[pl.ds(n * 8, 8)], gw.at[pl.ds(n * 8, 8)], osem.at[n]
        )

    def group(n, carry):
        group8 = pl.ds(n * 8, 8)
        pltpu.make_async_copy(gwd.at[group8], gbuf.at[group8], gsem.at[n]).wait()
        for m in range(8):
            s = n * 8 + m
            alive = (s < count[0, 0]).astype(F32)
            obuf[s] = gbuf[s].astype(F32) * alive
        flush(n).start()
        return carry

    lax.fori_loop(0, CAP // 8, group, 0)
    for d, e in zip(ins, outs):
        d.wait()
        e.start()

    def done(n, carry):
        flush(n).wait()
        return carry

    lax.fori_loop(0, CAP // 8, done, 0)
    for e in outs:
        e.wait()


def per_device(tokens, weight_blocks, block_rows, block_cols, block_count, grad_act):
    vmem = pl.BlockSpec(memory_space=pltpu.VMEM)
    smem = pl.BlockSpec(memory_space=pltpu.SMEM)
    hbm = pl.BlockSpec(memory_space=pl.ANY)
    rows, cols, count = block_rows[0, 0], block_cols[0, 0], block_count
    act_shape = jax.ShapeDtypeStruct((64, CBK * BLK), BF16)
    dx_shape = jax.ShapeDtypeStruct((BLK, RB * BLK), F32)
    act, dx, gwd = pl.pallas_call(
        kernel,
        out_shape=(
            act_shape,
            dx_shape,
            jax.ShapeDtypeStruct((RB * CBK, BLK, BLK), BF16),
        ),
        in_specs=[smem, smem, smem, hbm, hbm, hbm],
        out_specs=(hbm, vmem, hbm),
        scratch_shapes=[
            pltpu.SMEM((8, BLK), jnp.int32),
            pltpu.VMEM((8, BLK), jnp.int32),
            pltpu.VMEM((CAP + 1, BLK, BLK), BF16),
            pltpu.VMEM((8, BLK, RB * BLK), BF16),
            pltpu.VMEM((RB * BLK, 1024), BF16),
            pltpu.VMEM((SL, 2, 4, 4, 64, W), BF16),
            pltpu.VMEM((SL, 2, 2, 2, 64, W), BF16),
            pltpu.VMEM((SL, 2, 2, 4, 64, W), BF16),
            pltpu.VMEM((SL, 2, 4, 64, W), BF16),
            pltpu.VMEM((SL, 2, 2, 32, W), BF16),
            pltpu.VMEM((SL, 2, 2, 64, W), BF16),
            pltpu.VMEM((NCH, 2, 4, 4, 64, W), BF16),
            pltpu.VMEM((8, BLK, RB * BLK), F32),
            pltpu.VMEM((64, CBK * BLK), BF16),
            pltpu.VMEM((SL, 2, 64, W), BF16),
            pltpu.VMEM((2, RB, 2 * WB, BLK, BLK), BF16),
            pltpu.VMEM((4, BLK, RB * BLK), BF16),
            pltpu.VMEM((4, BLK, RB * BLK), BF16),
            pltpu.VMEM((4, BLK, RB * BLK), BF16),
            pltpu.VMEM((2, 64, RB * BLK), BF16),
            pltpu.VMEM((2, BLK, RB * BLK), BF16),
            pltpu.SemaphoreType.DMA((SL, 2, 4)),
            pltpu.SemaphoreType.DMA((SL, 2, 12)),
            pltpu.SemaphoreType.DMA((2,)),
            pltpu.SemaphoreType.DMA((23,)),
            pltpu.SemaphoreType.DMA((4,)),
            pltpu.SemaphoreType.DMA((SL, 2)),
            pltpu.SemaphoreType.DMA((2, RB)),
        ],
        compiler_params=pltpu.CompilerParams(
            collective_id=0, has_side_effects=True, vmem_limit_bytes=67043328
        ),
        name="ffn",
    )(rows, cols, count, tokens, weight_blocks[0, 0], grad_act)
    act, dx, gw = pl.pallas_call(
        pick_kernel,
        out_shape=(act_shape, dx_shape, jax.ShapeDtypeStruct((CAP, BLK, BLK), F32)),
        in_specs=[smem, smem, smem, hbm, hbm, hbm],
        out_specs=(hbm, hbm, hbm),
        scratch_shapes=[
            pltpu.VMEM(act_shape.shape, BF16),
            pltpu.VMEM(dx_shape.shape, F32),
            pltpu.VMEM((CAP, BLK, BLK), BF16),
            pltpu.VMEM((CAP, BLK, BLK), F32),
            pltpu.SemaphoreType.DMA((4,)),
            pltpu.SemaphoreType.DMA((CAP // 8,)),
            pltpu.SemaphoreType.DMA((CAP // 8,)),
        ],
        compiler_params=pltpu.CompilerParams(vmem_limit_bytes=67043328),
        name="pick",
    )(rows, cols, count, act, dx, gwd)
    return (act, dx, gw[None, None])


def solution(mesh):
    in_specs = (
        P("outb", "inb"),
        P("inb", "outb", None, None, None),
        P("inb", "outb", None),
        P("inb", "outb", None),
        P("inb", "outb"),
        P("inb", "outb"),
    )
    out_specs = (P("inb", "outb"), P("outb", "inb"), P("inb", "outb", None, None, None))
    return jax.shard_map(
        per_device, mesh=mesh, in_specs=in_specs, out_specs=out_specs, check_vma=False
    )
```

```python
import functools

import jax
import jax.numpy as jnp
from jax import lax
from jax.experimental import pallas as pl
from jax.experimental.pallas import tpu as pltpu
from jax.sharding import PartitionSpec as P

MESH = pl.DeviceIdType.MESH
F32 = jnp.float32
BF16 = jnp.bfloat16
INV_ROOT_TWO = 0.7071067811865476
INV_ROOT_TAU = 0.3989422804014327
BLK = 128
RB = 6
CBK = 48
CAP = 72
WB = 3
W = WB * BLK
NCH = CBK // (2 * WB)
SL = 4
EARLY = 1


def add2(a, b):
    return (a.astype(F32) + b.astype(F32)).astype(BF16)


def kernel(
    rows_in, cols_in, count_in, tok, wblk, gact_hbm,
    act_hbm, dx_out, gw_hbm,
    idx, tbl,
    wp, xs, xt, ps, r1, r2, qs, t1, t2, gs, dxa, gact, act, gwst, sb, sr, eb, u1, u2,
    ssem, rsem, asem, arsem, lsem, osem, gsem,
):
    a = lax.axis_index("inb")
    b = lax.axis_index("outb")
    x, y = a // 4, a % 4
    z, c = b // 2, b % 2

    def up(v):
        return lax.rem(v + 1, 4)

    def down(v):
        return lax.rem(v + 3, 4)

    def opp(v):
        return lax.rem(v + 2, 4)

    zr, zl = up(z), down(z)
    sib = (a, 2 * z + (1 - c))
    zr_dev, zl_dev = (a, 2 * zr + c), (a, 2 * zl + c)

    xr = lax.rem(x - z + 5, 4)
    first = (xr, y)
    second = (y, xr)

    def dev_x(v):
        return (4 * lax.rem(v + z + 3, 4) + y, b)

    def dev_y(v):
        return (4 * x + v, b)

    def dev_first(t, v):
        return dev_x(v) if t == 0 else dev_y(v)

    def dev_second(t, v):
        return dev_y(v) if t == 0 else dev_x(v)

    wcopy = pltpu.make_async_copy(wblk, wp.at[pl.ds(0, CAP)], lsem.at[0])
    wcopy.start()
    xcopy = pltpu.make_async_copy(tok, xs.at[2 + c], lsem.at[1])
    xcopy.start()
    gcopy = pltpu.make_async_copy(gact_hbm, gact, lsem.at[2])
    gcopy.start()

    barrier = pltpu.get_barrier_semaphore()
    for dev in (
        dev_x(up(xr)), dev_x(down(xr)), dev_y(up(y)), dev_y(down(y)),
        zr_dev, zl_dev, sib,
    ):
        pl.semaphore_signal(barrier, inc=1, device_id=dev, device_id_type=MESH)
    wp[CAP] = jnp.zeros((BLK, BLK), BF16)

    flat = BLK * lax.broadcasted_iota(jnp.int32, (8, BLK), 0) + lax.broadcasted_iota(jnp.int32, (8, BLK), 1)

    def place(n, found):
        cell = (rows_in[n] - a * RB) * CBK + cols_in[n] - b * CBK
        cell = jnp.where(n < count_in[0, 0], cell, 8 * BLK)
        return jnp.where(flat == cell, n, found)

    tbl[...] = lax.fori_loop(0, CAP, place, jnp.full((8, BLK), CAP, jnp.int32), unroll=4)
    tcopy = pltpu.make_async_copy(tbl, idx, lsem.at[3])
    tcopy.start()
    pl.semaphore_wait(barrier, 7)

    def ac(part, n, src, dst, dev):
        return pltpu.make_async_remote_copy(
            src_ref=src, dst_ref=dst, send_sem=asem.at[part], recv_sem=arsem.at[n],
            device_id=dev, device_id_type=MESH,
        )

    def go(part, n, src, dst, dev):
        ac(part, n, src, dst, dev).start()

    def got(n, dst):
        ac(0, n, dst, dst, sib).wait_recv()

    def xq(j, cc, h):
        return xs.at[2 * j + cc, pl.ds(32 * h, 32)]

    xcopy.wait()
    for n in range(4):
        m = (n + 2) % 4
        go(0, n, xq(1, c, n), xq(0, c, n), zr_dev)
        go(0, 4 + m, xq(1, c, m), xq(2, c, m), zl_dev)
    go(0, 8, xs.at[2 + c], xs.at[2 + c], sib)
    dxa[...] = jnp.zeros_like(dxa)
    wcopy.wait()
    tcopy.wait()
    got(8, xs.at[2 + 1 - c])

    def weights(k):
        cols = []
        for j in range(2 * WB):
            col = 2 * WB * k + j
            cols.append(jnp.concatenate([wp[idx[(r * CBK + col) // BLK, (r * CBK + col) % BLK]] for r in range(RB)], axis=0))
        return jnp.concatenate(cols, axis=1)

    def copy(k, t, part, n, src, dst, dev):
        slot = lax.rem(k, SL)
        return pltpu.make_async_remote_copy(
            src_ref=src, dst_ref=dst,
            send_sem=ssem.at[slot, t, part], recv_sem=rsem.at[slot, t, n],
            device_id=dev, device_id_type=MESH,
        )

    def start(k, t, n, src, dst, dev):
        copy(k, t, n // 3, n, src, dst, dev).start()

    def arrived(k, t, n, dst):
        copy(k, t, n // 3, n, dst, dst, sib).wait_recv()

    def sent(k, t, part, src):
        copy(k, t, part, 3 * part, src, src, sib).wait_send()

    def rows(slot, m, rhs):
        lhs = jnp.concatenate([xs[2 * m], xs[2 * m + 1]], axis=0)
        out = jnp.dot(lhs, rhs, preferred_element_type=F32).astype(BF16)
        for n in range(4):
            ps[slot, 0, m, n] = out[64 * n:64 * n + 64, :W]
            ps[slot, 1, n, m] = out[64 * n:64 * n + 64, W:]

    def stage0(k):
        rhs = weights(k)
        for m in range(4):
            rows(lax.rem(k, SL), m, rhs)
        send0(k)

    def send0(k):
        slot = lax.rem(k, SL)
        for t in range(2):
            f = first[t]
            r, l, o = up(f), down(f), opp(f)
            lo, hi = pl.ds(0, 2), pl.ds(2, 2)
            start(k, t, 0, ps.at[slot, t, o, lo], r1.at[slot, t, 0], dev_first(t, r))
            start(k, t, 1, ps.at[slot, t, o, hi], r1.at[slot, t, 1], dev_first(t, l))
            start(k, t, 2, ps.at[slot, t, r, hi], r2.at[slot, t, 0, hi], dev_first(t, r))
            start(k, t, 2, ps.at[slot, t, l, lo], r2.at[slot, t, 1, lo], dev_first(t, l))

    def stage1(k):
        slot = lax.rem(k, SL)
        for t in range(2):
            f = first[t]
            r, l = up(f), down(f)
            lo, hi = pl.ds(0, 2), pl.ds(2, 2)
            arrived(k, t, 0, r1.at[slot, t, 0])
            ps[slot, t, r, lo] = add2(ps[slot, t, r, lo], r1[slot, t, 0])
            start(k, t, 2, ps.at[slot, t, r, lo], r2.at[slot, t, 0, lo], dev_first(t, r))
            arrived(k, t, 1, r1.at[slot, t, 1])
            ps[slot, t, l, hi] = add2(ps[slot, t, l, hi], r1[slot, t, 1])
            start(k, t, 2, ps.at[slot, t, l, hi], r2.at[slot, t, 1, hi], dev_first(t, l))

    def stage2(k):
        slot = lax.rem(k, SL)
        for t in range(2):
            f, s = first[t], second[t]
            arrived(k, t, 2, r2.at[slot, t])
            qs[slot, t] = (
                ps[slot, t, f].astype(F32) + r2[slot, t, 0].astype(F32) + r2[slot, t, 1].astype(F32)
            ).astype(BF16)
            sent(k, t, 0, ps.at[slot, t, pl.ds(0, 3)])
            r, l, o = up(s), down(s), opp(s)
            lo, hi = pl.ds(0, 32), pl.ds(32, 32)
            start(k, t, 3, qs.at[slot, t, o, lo], t1.at[slot, t, 0], dev_second(t, r))
            start(k, t, 4, qs.at[slot, t, o, hi], t1.at[slot, t, 1], dev_second(t, l))

    def stage3(k):
        slot = lax.rem(k, SL)
        for t in range(2):
            s = second[t]
            r, l = up(s), down(s)
            lo, hi = pl.ds(0, 32), pl.ds(32, 32)
            arrived(k, t, 3, t1.at[slot, t, 0])
            qs[slot, t, r, lo] = add2(qs[slot, t, r, lo], t1[slot, t, 0])
            start(k, t, 5, qs.at[slot, t, r], t2.at[slot, t, 0], dev_second(t, r))
            arrived(k, t, 4, t1.at[slot, t, 1])
            qs[slot, t, l, hi] = add2(qs[slot, t, l, hi], t1[slot, t, 1])
            start(k, t, 5, qs.at[slot, t, l], t2.at[slot, t, 1], dev_second(t, l))

    def stage4(k):
        slot = lax.rem(k, SL)
        for t in range(2):
            f, s = first[t], second[t]
            arrived(k, t, 5, t2.at[slot, t])
            pre = qs[slot, t, s].astype(F32) + t2[slot, t, 0].astype(F32) + t2[slot, t, 1].astype(F32)
            cdf = 0.5 * (1.0 + lax.erf(pre * INV_ROOT_TWO))
            cols = pl.ds(pl.multiple_of((2 * k + t) * W, W), W)
            slope = cdf + pre * jnp.exp(-0.5 * pre * pre) * INV_ROOT_TAU
            gs[k, t, f, s] = (gact[:, cols].astype(F32) * slope).astype(BF16)
            sent(k, t, 1, qs.at[slot, t, pl.ds(0, 3)])
            start(k, t, 6, gs.at[k, t, f, s], gs.at[k, t, f, s], dev_second(t, up(s)))
            start(k, t, 7, gs.at[k, t, f, s], gs.at[k, t, f, s], dev_second(t, down(s)))

            @pl.when(k >= SL)
            def _():
                pltpu.make_async_copy(act.at[slot, t], act_hbm.at[:, cols], osem.at[slot, t]).wait()

            act[slot, t] = (pre * cdf).astype(BF16)
            pltpu.make_async_copy(act.at[slot, t], act_hbm.at[:, cols], osem.at[slot, t]).start()

    def stage5(k):
        for t in range(2):
            f, s = first[t], second[t]
            r, l = up(s), down(s)
            lo, hi = pl.ds(0, 32), pl.ds(32, 32)
            arrived(k, t, 6, gs.at[k, t, f, l])
            start(k, t, 8, gs.at[k, t, f, l, lo], gs.at[k, t, f, l, lo], dev_second(t, r))
            arrived(k, t, 7, gs.at[k, t, f, r])
            start(k, t, 8, gs.at[k, t, f, r, hi], gs.at[k, t, f, r, hi], dev_second(t, l))

    def stage6(k):
        for t in range(2):
            f, s = first[t], second[t]
            arrived(k, t, 8, gs.at[k, t, f, opp(s)])
            start(k, t, 9, gs.at[k, t, f], gs.at[k, t, f], dev_first(t, up(f)))
            start(k, t, 10, gs.at[k, t, f], gs.at[k, t, f], dev_first(t, down(f)))

    def stage7(k):
        for t in range(2):
            f = first[t]
            r, l = up(f), down(f)
            lo, hi = pl.ds(0, 2), pl.ds(2, 2)
            sent(k, t, 2, gs.at[k, t, f, pl.ds(0, 3)])
            arrived(k, t, 9, gs.at[k, t, l])
            start(k, t, 11, gs.at[k, t, l, lo], gs.at[k, t, l, lo], dev_first(t, r))
            arrived(k, t, 10, gs.at[k, t, r])
            start(k, t, 11, gs.at[k, t, r, hi], gs.at[k, t, r, hi], dev_first(t, l))

    def gw_copies(k):
        g = lax.rem(k, 2)
        return [
            pltpu.make_async_copy(
                gwst.at[g, r], gw_hbm.at[pl.ds(r * CBK + 2 * WB * k, 2 * WB)], gsem.at[g, r]
            )
            for r in range(RB)
        ]

    def arrive8(k):
        for t in range(2):
            f = first[t]
            arrived(k, t, 11, gs.at[k, t, opp(f)])
            sent(k, t, 3, gs.at[k, t, pl.ds(0, 3)])

    def whole_g(k):
        g0 = jnp.concatenate([gs[k, 0, n // 4, n % 4] for n in range(16)], axis=0)
        g1 = jnp.concatenate([gs[k, 1, n % 4, n // 4] for n in range(16)], axis=0)
        return jnp.concatenate([g0, g1], axis=1)

    def slot_grads(k, g):
        @pl.when(k >= 2)
        def _():
            for d in gw_copies(k - 2):
                d.wait()

        wg = jnp.dot(xt[...], g, preferred_element_type=F32).astype(BF16)
        for r in range(RB):
            for j in range(2 * WB):
                gwst[lax.rem(k, 2), r, j] = wg[r * BLK:(r + 1) * BLK, j * BLK:(j + 1) * BLK]
        for d in gw_copies(k):
            d.start()

    def stage8(k):
        arrive8(k)
        g = whole_g(k)
        term = lax.dot_general(
            g, weights(k), (((1,), (1,)), ((), ())), preferred_element_type=F32
        )
        dxa[...] += term.reshape(8, BLK, RB * BLK)
        slot_grads(k, g)

    stages = (stage0, stage1, stage2, stage3, stage4, stage5, stage6, stage7, stage8)

    def early(j):
        for k in range(EARLY):
            rows(k, j, weights(k))

    for n in range(2):
        got(n, xq(0, c, n))
        go(0, 9 + n, xq(0, c, n), xq(3, c, n), zr_dev)
        got(6 + n, xq(2, c, n + 2))
        go(0, 11 + n, xq(2, c, n + 2), xq(3, c, n + 2), zl_dev)
        go(0, 13, xq(0, c, n), xq(0, c, n), sib)
        go(0, 14, xq(2, c, n + 2), xq(2, c, n + 2), sib)
    for n in range(2):
        got(2 + n, xq(0, c, n + 2))
        go(0, 13, xq(0, c, n + 2), xq(0, c, n + 2), sib)
        got(4 + n, xq(2, c, n))
        go(0, 14, xq(2, c, n), xq(2, c, n), sib)
    early(1)
    for n in range(2):
        got(9 + n, xq(3, c, n))
        go(0, 15, xq(3, c, n), xq(3, c, n), sib)
        got(11 + n, xq(3, c, n + 2))
        go(0, 15, xq(3, c, n + 2), xq(3, c, n + 2), sib)
    got(13, xs.at[1 - c])
    early(0)
    got(14, xs.at[4 + 1 - c])
    early(2)
    got(15, xs.at[6 + 1 - c])
    early(3)
    for k in range(EARLY):
        send0(k)
    ac(0, 0, xs.at[pl.ds(0, 7)], xs.at[pl.ds(0, 7)], sib).wait_send()
    gcopy.wait()

    def body(i, carry):
        for n in (7, 6, 5, 4, 3, 2, 1, 0, 8):
            k = i - n

            @pl.when((k >= (0 if n else EARLY)) & (k < NCH))
            def _():
                stages[n](k)

        @pl.when(i == 6)
        def _():
            for r in range(RB):
                for q in range(8):
                    xt[r * BLK:(r + 1) * BLK, q * BLK:(q + 1) * BLK] = xs[q, :, r * BLK:(r + 1) * BLK].T

        return carry

    lax.fori_loop(1, NCH + len(stages) - 2, body, 0)

    last = NCH - 1
    arrive8(last)
    rhs = weights(last)
    for q in (3, 2, 0, 1):
        g0 = jnp.concatenate([gs[last, 0, q, m] for m in range(4)], axis=0)
        g1 = jnp.concatenate([gs[last, 1, m, q] for m in range(4)], axis=0)
        g = jnp.concatenate([g0, g1], axis=1)
        term = lax.dot_general(g, rhs, (((1,), (1,)), ((), ())), preferred_element_type=F32)
        dxa[2 * q:2 * q + 2] += term.reshape(2, BLK, RB * BLK)
        sb[q] = dxa[2 * q + (1 - c)].astype(BF16)
        go(1, 16 + q, sb.at[q], sr.at[q], sib)
    lo, hi = pl.ds(0, 64), pl.ds(64, 64)

    def join(q):
        got(16 + q, sr.at[q])
        eb[q] = (dxa[2 * q + c] + sr[q].astype(F32)).astype(BF16)

    join(3)
    go(1, 20, eb.at[3, lo], u1.at[0], zr_dev)
    go(1, 21, eb.at[3, hi], u1.at[1], zl_dev)
    join(2)
    go(1, 22, eb.at[2, hi], u2.at[0, hi], zr_dev)
    join(0)
    go(1, 22, eb.at[0, lo], u2.at[1, lo], zl_dev)
    join(1)
    got(20, u1.at[0])
    eb[2, lo] = add2(eb[2, lo], u1[0])
    go(1, 22, eb.at[2, lo], u2.at[0, lo], zr_dev)
    got(21, u1.at[1])
    eb[0, hi] = add2(eb[0, hi], u1[1])
    go(1, 22, eb.at[0, hi], u2.at[1, hi], zl_dev)
    slot_grads(last, whole_g(last))
    for k in range(NCH - SL, NCH):
        for t in range(2):
            cols = pl.ds((2 * k + t) * W, W)
            pltpu.make_async_copy(
                act.at[k % SL, t], act_hbm.at[:, cols], osem.at[k % SL, t]
            ).wait()
    for k in (last - 1, last):
        for d in gw_copies(k):
            d.wait()
    got(22, u2)
    dx_out[...] = eb[1].astype(F32) + u2[0].astype(F32) + u2[1].astype(F32)
    ac(1, 0, xs.at[pl.ds(0, 7)], xs.at[pl.ds(0, 7)], sib).wait_send()


def pick_kernel(rows, cols, count, act_in, dx_in, gwd, act, dx, gw, abuf, dbuf, gbuf, obuf, sem, gsem, osem):
    row0 = lax.axis_index("inb") * RB
    col0 = lax.axis_index("outb") * CBK

    def fetch(s):
        cell = (rows[s] - row0) * CBK + cols[s] - col0
        return pltpu.make_async_copy(gwd.at[cell], gbuf.at[s], gsem.at[s // 8])

    def begin(s, carry):
        fetch(s).start()
        return carry

    lax.fori_loop(0, CAP, begin, 0, unroll=4)
    ins = [
        pltpu.make_async_copy(act_in, abuf, sem.at[0]),
        pltpu.make_async_copy(dx_in, dbuf, sem.at[1]),
    ]
    for d in ins:
        d.start()
    outs = [
        pltpu.make_async_copy(abuf, act, sem.at[2]),
        pltpu.make_async_copy(dbuf, dx, sem.at[3]),
    ]

    def flush(n):
        return pltpu.make_async_copy(
            obuf.at[pl.ds(n * 8, 8)], gw.at[pl.ds(n * 8, 8)], osem.at[n]
        )

    def group(n, carry):
        group8 = pl.ds(n * 8, 8)
        pltpu.make_async_copy(gwd.at[group8], gbuf.at[group8], gsem.at[n]).wait()
        for m in range(8):
            s = n * 8 + m
            alive = (s < count[0, 0]).astype(F32)
            obuf[s] = gbuf[s].astype(F32) * alive
        flush(n).start()
        return carry

    lax.fori_loop(0, CAP // 8, group, 0)
    for d, e in zip(ins, outs):
        d.wait()
        e.start()

    def done(n, carry):
        flush(n).wait()
        return carry

    lax.fori_loop(0, CAP // 8, done, 0)
    for e in outs:
        e.wait()


def per_device(tokens, weight_blocks, block_rows, block_cols, block_count, grad_act):
    vmem = pl.BlockSpec(memory_space=pltpu.VMEM)
    smem = pl.BlockSpec(memory_space=pltpu.SMEM)
    hbm = pl.BlockSpec(memory_space=pl.ANY)
    rows, cols, count = block_rows[0, 0], block_cols[0, 0], block_count
    act_shape = jax.ShapeDtypeStruct((64, CBK * BLK), BF16)
    dx_shape = jax.ShapeDtypeStruct((BLK, RB * BLK), F32)
    act, dx, gwd = pl.pallas_call(
        kernel,
        out_shape=(
            act_shape,
            dx_shape,
            jax.ShapeDtypeStruct((RB * CBK, BLK, BLK), BF16),
        ),
        in_specs=[smem, smem, smem, hbm, hbm, hbm],
        out_specs=(hbm, vmem, hbm),
        scratch_shapes=[
            pltpu.SMEM((8, BLK), jnp.int32),
            pltpu.VMEM((8, BLK), jnp.int32),
            pltpu.VMEM((CAP + 1, BLK, BLK), BF16),
            pltpu.VMEM((8, BLK, RB * BLK), BF16),
            pltpu.VMEM((RB * BLK, 1024), BF16),
            pltpu.VMEM((SL, 2, 4, 4, 64, W), BF16),
            pltpu.VMEM((SL, 2, 2, 2, 64, W), BF16),
            pltpu.VMEM((SL, 2, 2, 4, 64, W), BF16),
            pltpu.VMEM((SL, 2, 4, 64, W), BF16),
            pltpu.VMEM((SL, 2, 2, 32, W), BF16),
            pltpu.VMEM((SL, 2, 2, 64, W), BF16),
            pltpu.VMEM((NCH, 2, 4, 4, 64, W), BF16),
            pltpu.VMEM((8, BLK, RB * BLK), F32),
            pltpu.VMEM((64, CBK * BLK), BF16),
            pltpu.VMEM((SL, 2, 64, W), BF16),
            pltpu.VMEM((2, RB, 2 * WB, BLK, BLK), BF16),
            pltpu.VMEM((4, BLK, RB * BLK), BF16),
            pltpu.VMEM((4, BLK, RB * BLK), BF16),
            pltpu.VMEM((4, BLK, RB * BLK), BF16),
            pltpu.VMEM((2, 64, RB * BLK), BF16),
            pltpu.VMEM((2, BLK, RB * BLK), BF16),
            pltpu.SemaphoreType.DMA((SL, 2, 4)),
            pltpu.SemaphoreType.DMA((SL, 2, 12)),
            pltpu.SemaphoreType.DMA((2,)),
            pltpu.SemaphoreType.DMA((23,)),
            pltpu.SemaphoreType.DMA((4,)),
            pltpu.SemaphoreType.DMA((SL, 2)),
            pltpu.SemaphoreType.DMA((2, RB)),
        ],
        compiler_params=pltpu.CompilerParams(
            collective_id=0, has_side_effects=True, vmem_limit_bytes=67043328
        ),
        name="ffn",
    )(rows, cols, count, tokens, weight_blocks[0, 0], grad_act)
    act, dx, gw = pl.pallas_call(
        pick_kernel,
        out_shape=(act_shape, dx_shape, jax.ShapeDtypeStruct((CAP, BLK, BLK), F32)),
        in_specs=[smem, smem, smem, hbm, hbm, hbm],
        out_specs=(hbm, hbm, hbm),
        scratch_shapes=[
            pltpu.VMEM(act_shape.shape, BF16),
            pltpu.VMEM(dx_shape.shape, F32),
            pltpu.VMEM((CAP, BLK, BLK), BF16),
            pltpu.VMEM((CAP, BLK, BLK), F32),
            pltpu.SemaphoreType.DMA((4,)),
            pltpu.SemaphoreType.DMA((CAP // 8,)),
            pltpu.SemaphoreType.DMA((CAP // 8,)),
        ],
        compiler_params=pltpu.CompilerParams(vmem_limit_bytes=67043328),
        name="pick",
    )(rows, cols, count, act, dx, gwd)
    return (act, dx, gw[None, None])


def solution(mesh):
    in_specs = (
        P("outb", "inb"),
        P("inb", "outb", None, None, None),
        P("inb", "outb", None),
        P("inb", "outb", None),
        P("inb", "outb"),
        P("inb", "outb"),
    )
    out_specs = (P("inb", "outb"), P("outb", "inb"), P("inb", "outb", None, None, None))
    return jax.shard_map(
        per_device, mesh=mesh, in_specs=in_specs, out_specs=out_specs, check_vma=False
    )
```
